512 devices in a mesh: group: 8 (over y), mesh: 32 (over z, x), comp: 2 (over core).
Axes of the slice: x: 4, y: 8, z: 8, core: 2. Of those that a mesh axis runs over, the one named last changes fastest.
Arguments:
- log_sigma: float32 [2048, 128], P('mesh'), may hold values from -1 to 1
- block_owner: int32 [8, 4096, 1], P('group', 'mesh'), may hold values from 0 to 31; in each aligned block of 128 rows (0 to 127, 128 to 255, ..., all dimensions but the last counted through in order) at most 8 rows name the same one
- block_slot: int32 [8, 4096], P('group', 'mesh'), may hold values from 0 to 63
- coupling: float32 [128, 128], replicated, may hold values from -0.6 to 10, as said below
- sources: float32 [8, 2, 8, 4096, 128], P('group', 'comp', None, 'mesh'), may hold values from -24 to 24
- rcv_cell: int32 [8, 4096], P('group', 'mesh'), may hold values from 0 to 16383
- observed: float32 [8, 2, 8, 4096], P('group', 'comp', None, 'mesh'), may hold values from -6 to 6
Outputs:
- gradient: float32 [2048, 128], P('mesh')
The draws below stay inside these ranges and needn't reach their ends.
Inputs may be any that keep to these rules, and one draw needn't show every extreme that they name: `block_owner`: in the 128 rows of one device of a group, no owner is named more than 8 times; some owner is named exactly 8 times in some device's rows. `rcv_cell`: A receiver's cell counts from the first cell of the modelling section of the device that holds the receiver's entry. `coupling`: every diagonal entry is 6 or more.
All inputs are finite; a program needn't handle non-finite values.
Results may differ from the reference program's by a relative error of at most 0.0003.
Values sent between devices are 32-bit elements; how exact they have to be, the bound alone decides.
A program may use at most 64 MiB of HBM per device.

```python
import math
import jax
import jax.numpy as jnp
import numpy as np
from jax import lax

CELLS = 128
S = 8
ITERS = 6
MB_DEV = 128
IB_DEV = 64
R_DEV = 128
GROUPS = 8
MB = 4096
NB_INV = 2048
RCV = 4096
CAP = 8
N_MESH = 32


def draw_coupling(key, part):
    diag_key, off_key = jax.random.split(jax.random.fold_in(key, 11))
    identity = jnp.arange(CELLS)[:, None] == jnp.arange(CELLS)[None, :]
    diagonal = jax.random.uniform(diag_key, (CELLS, CELLS), jnp.float32, 6.0, 10.0)
    offdiag = jnp.clip(0.15 * jax.random.normal(off_key, (CELLS, CELLS), jnp.float32), -0.6, 0.6)
    return jnp.where(identity, diagonal, offdiag)


def place_ends(result, key, low, high):
    longest = result.shape.index(max(result.shape))
    spots = []
    for shift in (0, 1):
        where = [jax.random.randint(jax.random.fold_in(key, axis), (), 0, length) for axis, length in enumerate(result.shape)]
        where[longest] = (where[longest] + shift) % result.shape[longest]
        spots.append(tuple(where))
    return result.at[spots[0]].set(low).at[spots[1]].set(high)


def levels(rng, dims, cuts, smallest, high):
    gain = 1.0
    for position, shards_of in cuts:
        steps = jax.random.uniform(jax.random.fold_in(jax.random.fold_in(rng, 6), position), (shards_of,), jnp.float32, smallest / len(cuts), high / len(cuts))
        gain = gain * jnp.repeat(jnp.exp(steps), dims[position] // shards_of).reshape((-1,) + (1,) * (len(dims) - 1 - position))
    return gain


def shared_out(rng, own, number, rows, amount, top, bound, slope):
    order = jax.random.permutation(rng, amount)
    crowded, usual = load_shares(amount, rows * top, bound, slope, True), load_shares(amount, rows * top, bound, slope, False)
    places = jnp.arange(amount)

    def named(lengths, turn):
        used = int((lengths > 0).sum())
        fixed = max(1, used // 4)
        passed = fixed + (places - fixed + turn * (used - fixed)) % max(1, amount - fixed)
        return jnp.zeros((amount,), jnp.int32).at[order[jnp.where(places < fixed, places, passed)]].set(jnp.asarray(lengths, jnp.int32))

    lengths = jnp.where(number % 4 == 0, named(crowded, number // 4), named(usual, number - number // 4 - 1))
    mixed = jax.random.permutation(jax.random.fold_in(own, 3), amount)
    donor, sink = mixed[0:amount // 2 * 2:2], mixed[1:amount // 2 * 2:2]
    slack = jnp.minimum(lengths[donor] - 1, bound - lengths[sink]) // 2
    slack = jnp.where((donor == order[0]) | (sink == order[0]) | (lengths[sink] == 0), 0, jnp.maximum(slack, 0))
    passed = jax.random.randint(jax.random.fold_in(own, 4), (amount // 2,), 0, 1 << 20) % (slack + 1)
    lengths = lengths.at[donor].add(-passed).at[sink].add(passed)
    labels = jnp.searchsorted(jnp.cumsum(lengths), jnp.arange(rows * top), side="right").astype(jnp.int32)
    listing = labels.reshape(top, rows).T
    listing = listing[jax.random.permutation(jax.random.fold_in(own, 1), rows)]
    turn = jax.random.randint(jax.random.fold_in(own, 2), (rows, 1), 0, top)
    return jnp.take_along_axis(listing, (jnp.arange(top)[None, :] + turn) % top, axis=1)


def load_shares(amount, total, limit, lean, full):
    portions = [(1 << 20) // math.isqrt(rank ** lean) + 1 for rank in range(1, amount + 1)]
    largest = limit if full else min(limit, max(-(-total // amount), total * portions[0] // sum(portions)))
    least = 1 if total - largest >= amount - 1 else 0
    holding, spare = [largest] + [least] * (amount - 1), total - largest - least * (amount - 1)
    while spare > 0:
        free = [i for i in range(1, amount) if holding[i] < largest] or [i for i in range(1, amount) if holding[i] < limit]
        mass, remaining = sum([portions[i] for i in free]), spare
        for i in free:
            extra = min(limit - holding[i], max(1, remaining * portions[i] // mass), spare)
            holding[i] = holding[i] + extra
            spare = spare - extra
    return np.array(holding)


def centred(rng, shape, width, reach, shards=(), held_as=jnp.bfloat16):
    gain = levels(rng, shape, shards, -0.22, 0.18) if shards else 1.0
    result = jax.random.normal(rng, shape, jnp.float32) * width * gain
    return jnp.minimum(jnp.maximum(result, -reach), reach).astype(held_as)


def setup_inputs(seed: int = 0) -> dict:
    keys = jax.random.split(jax.random.key(seed), 8)
    log_sigma = jnp.clip(jax.random.uniform(keys[0], (NB_INV, CELLS), jnp.float32, -1.0, 1.0) * levels(keys[0], (NB_INV, CELLS), ((0, 32),), -0.4, 0.0), -1.0, 1.0)
    block_owner_keys = jax.random.split(jax.random.fold_in(keys[1], 1), GROUPS * MB // MB_DEV)
    block_owner_turns = jax.random.permutation(jax.random.fold_in(keys[1], 3), GROUPS * MB // MB_DEV)
    block_owner = jax.vmap(lambda own, number: shared_out(jax.random.fold_in(keys[1], 2), own, number, MB_DEV, N_MESH, 1, CAP, 2))(block_owner_keys, block_owner_turns).reshape((GROUPS, MB, 1))
    block_slot = place_ends(jax.random.randint(keys[2], (GROUPS, MB), 0, IB_DEV), jax.random.fold_in(keys[2], 1), 0, IB_DEV - 1).astype(jnp.int32)
    coupling = draw_coupling(jax.random.fold_in(keys[7], 71), 0)
    sources = centred(keys[4], (GROUPS, 2, S, MB, CELLS), 4.0, 24.0, ((0, 8), (1, 2), (3, 32)), jnp.float32)
    rcv_cell = place_ends(jax.random.randint(keys[5], (GROUPS, RCV), 0, MB_DEV * CELLS), jax.random.fold_in(keys[5], 1), 0, (MB_DEV * CELLS) - 1).astype(jnp.int32)
    observed = centred(keys[6], (GROUPS, 2, S, RCV), 1.0, 6.0, ((0, 8), (1, 2), (3, 32)), jnp.float32)
    return dict(log_sigma=log_sigma, block_owner=block_owner, block_slot=block_slot, coupling=coupling, sources=sources, rcv_cell=rcv_cell, observed=observed)


omega_freq = 0.8
chain_weight = 1.0


def block_product(values, matrix):
    shaped = values.reshape(values.shape[:-1] + (-1, CELLS))
    product = jnp.einsum("...bj,ij->...bi", shaped, matrix, precision=lax.Precision.HIGHEST)
    return product.reshape(values.shape)


def neighbours(values):
    zero_cells = jnp.zeros(values.shape[:-1] + (1,), values.dtype)
    earlier = jnp.concatenate([zero_cells, values[..., :-1]], axis=-1)
    later = jnp.concatenate([values[..., 1:], zero_cells], axis=-1)
    return earlier + later


def operate(values, matrix, cross_coef):
    return block_product(values, matrix) - chain_weight * neighbours(values) + cross_coef * values[::-1]


def relax(right, matrix, cross_coef, inverse_diag):
    state = jnp.zeros_like(right)
    for iteration in range(ITERS):
        state = state + inverse_diag * (right - operate(state, matrix, cross_coef))
    return state


def reference(log_sigma, block_owner, block_slot, coupling, sources, rcv_cell, observed):
    inverse_diag = jnp.tile(1.0 / jnp.diagonal(coupling), MB_DEV * N_MESH)
    device_base = ((jnp.arange(R_DEV * N_MESH) // R_DEV) * (MB_DEV * CELLS)).astype(jnp.int32)

    def one_group(summed, inputs):
        owners, slots, group_src, group_rcv, group_obs = inputs
        inv_rows = (owners[:, 0] * IB_DEV + slots).astype(jnp.int32)
        sigmas = jnp.exp(jnp.take(log_sigma, inv_rows, axis=0)).reshape(-1)
        cross_coef = omega_freq * jnp.stack([-sigmas, sigmas])[:, None, :]
        right = group_src.reshape(2, S, -1)
        field_now = relax(right, coupling, cross_coef, inverse_diag)
        places = device_base + group_rcv.astype(jnp.int32)
        misfit = field_now[:, :, places] - group_obs
        adjoint_src = jnp.zeros_like(right).at[:, :, places].add(misfit)
        adjoint = relax(adjoint_src, coupling.T, -cross_coef, inverse_diag)
        weighted = jnp.sum(adjoint[0] * field_now[1] - adjoint[1] * field_now[0], axis=0)
        partial_rows = (omega_freq * sigmas * weighted).reshape(-1, CELLS)
        return summed.at[inv_rows].add(partial_rows), None

    start_sum = jnp.zeros(log_sigma.shape, jnp.float32)
    summed, unused = lax.scan(one_group, start_sum, (block_owner, block_slot, sources, rcv_cell, observed))
    return summed
```

```python
import functools

import jax
import jax.numpy as jnp
from jax import lax
from jax.experimental import pallas as pl
from jax.experimental.pallas import tpu as pltpu
from jax.sharding import PartitionSpec as P

CELLS = 128
S = 8
ITERS = 6
CAP = 8
NX = 4
BLOCKS = 128
HALO = 8
HALF = (BLOCKS + 2 * HALO) // 2
ROWS = HALF * 8
STAGE = BLOCKS + 2 * HALO
OWNED = 64
OMEGA = 0.8
CHAIN = 1.0

f32, bf16, i32 = jnp.float32, jnp.bfloat16, jnp.int32
NT = (((1,), (1,)), ((), ()))


def iota(shape, dim):
    return lax.broadcasted_iota(i32, shape, dim)


def two(x):
    hi = x.astype(bf16)
    return hi, (x - hi.astype(f32)).astype(bf16)


def three(x):
    hi = x.astype(bf16)
    rest = x - hi.astype(f32)
    mid = rest.astype(bf16)
    return hi, mid, (rest - mid.astype(f32)).astype(bf16)


def dot(a, b):
    return jnp.dot(a, b, preferred_element_type=f32)


def dot_t(a, b):
    return lax.dot_general(a, b, NT, preferred_element_type=f32)


def column(row):
    n = row.shape[1]
    return jnp.sum(jnp.where(iota((n, n), 0) == iota((n, n), 1), row, 0.0), axis=1, keepdims=True)


def kernel(
    ng, nm, t_ref, rcv_ref, obs_ref, cpl_ref, ls_ref, src_ref, out_ref,
    stage, table, tn, rn, obs_own, obs_near, index_v, index_s, picked, theirs, choose,
    x_buf, lhs, mm, q, cross, wsig, hits, heard, count, wf, wa, qmat, psum_buf, part,
    slots, slots_in, pack, pack_in, grad, grad_in, line, total, total_in,
    local_sem, ex_send, ex_recv, halo_send, halo_recv, small_send, small_recv,
    ag_send, ag_recv, fan_send, pick_send, pick_recv, sl_send, sl_recv, gp_send, gp_recv,
    gr_send, gr_recv, ln_send, ln_recv, to_send, to_recv, index_sem,
):
    me = lax.axis_index("mesh")
    core = lax.axis_index("comp")
    grp = lax.axis_index("group")
    other = 1 - core
    nz = nm // NX
    mz, mx = me // NX, me % NX
    right, left = (me + 1) % nm, (me + nm - 1) % nm

    def far_first(i, n):
        return (n // 2 + ((i + 1) // 2) * (1 - 2 * (i % 2)) + n) % n

    def mesh_at(i):
        dz, dx = far_first(i // NX, nz), far_first(i % NX, NX)
        return ((mz + dz) % nz) * NX + (mx + dx) % NX

    def remote(src, dst, ssem, rsem, **where):
        return pltpu.make_async_remote_copy(
            src_ref=src, dst_ref=dst, send_sem=ssem, recv_sem=rsem,
            device_id=where, device_id_type=pl.DeviceIdType.MESH,
        )

    barrier = pltpu.get_barrier_semaphore()

    def greet(**where):
        pl.semaphore_signal(barrier, inc=1, device_id=where, device_id_type=pl.DeviceIdType.MESH)

    @pl.loop(0, nm - 1)
    def _(i):
        greet(mesh=mesh_at(i))

    @pl.loop(1, ng)
    def _(d):
        greet(group=(grp + d) % ng)

    greet(comp=other)
    greet(mesh=left, comp=other)
    greet(mesh=right, comp=other)

    own_half = pl.ds(pl.multiple_of(core * (OWNED // 2), 8), OWNED // 2)
    half_rows = OWNED // 2

    def table_rows(owner):
        return table.at[pl.ds(pl.multiple_of(owner * half_rows, 8), half_rows), :]

    own_table = pltpu.make_async_copy(ls_ref.at[own_half, :], table_rows(me), local_sem.at[4])
    own_table.start()

    def stage_rows(p, s, first, n):
        return stage.at[pl.ds(pl.multiple_of(p * (4 * STAGE) + s * STAGE + first, 8), n), :]

    def own_copy(s):
        return pltpu.make_async_copy(
            src_ref.at[4 * core + s], stage_rows(core, s, HALO, BLOCKS), local_sem.at[s]
        )

    @pl.loop(0, 4)
    def _(s):
        own_copy(s).start()

    eye = iota((CELLS, CELLS), 0) == iota((CELLS, CELLS), 1)
    beside = jnp.abs(iota((CELLS, CELLS), 0) - iota((CELLS, CELLS), 1)) == 1
    cpl = cpl_ref[...]
    dinv = 1.0 / jnp.sum(jnp.where(eye, cpl, 0.0), axis=0, keepdims=True)
    for m, w in ((cpl.T, wf), (cpl, wa)):
        scaled = -dinv * (jnp.where(eye, 0.0, m) - jnp.where(beside, CHAIN, 0.0))
        hi, lo = two(scaled)
        w[0:CELLS, 0:CELLS] = hi
        w[0:CELLS, CELLS:] = lo
        w[CELLS:, 0:CELLS] = hi
        w[CELLS:, CELLS:] = lo

    pl.semaphore_wait(barrier, nm - 1 + ng - 1 + 3)

    def along_z(i):
        z = (mz + far_first(i, nz)) % nz
        return remote(ls_ref.at[own_half, :], table_rows(me), ag_send.at[i], ag_recv.at[me], mesh=z * NX + mx)

    @pl.loop(0, nz - 1)
    def _(i):
        along_z(i).start()

    def small(k, **where):
        return (
            remote(t_ref, tn.at[k], small_send.at[k, 0], small_recv.at[k, 0], **where),
            remote(rcv_ref, rn.at[k], small_send.at[k, 1], small_recv.at[k, 1], **where),
        )

    smalls = small(0, mesh=right) + small(1, mesh=left)
    for c in smalls:
        c.start()

    def exchange(s):
        return remote(
            src_ref.at[4 * other + s], stage_rows(core, s, HALO, BLOCKS), ex_send.at[s], ex_recv.at[s], comp=other
        )

    @pl.loop(0, 4)
    def _(s):
        exchange(s).start()

    def halo(side, c, s):
        first, into = (BLOCKS - HALO, 0) if side == 0 else (0, STAGE - HALO)
        return remote(
            src_ref.at[4 * c + s, pl.ds(first, HALO), :], stage_rows(core, s, into, HALO),
            halo_send.at[side, c, s], halo_recv.at[side, core, s],
            mesh=right if side == 0 else left, comp=c,
        )

    @pl.loop(0, 8)
    def _(k):
        halo(0, k // 4, k % 4).start()
        halo(1, k // 4, k % 4).start()

    def obs_to(side, c):
        return remote(
            obs_ref, obs_near.at[side, core], halo_send.at[side, c, 4], halo_recv.at[side, core, 4],
            mesh=right if side == 0 else left, comp=c,
        )

    @pl.loop(0, 2)
    def _(c):
        obs_to(0, c).start()
        obs_to(1, c).start()

    obs_swap = remote(obs_ref, obs_own.at[core], ex_send.at[4], ex_recv.at[4], comp=other)
    obs_swap.start()
    obs_own[core] = obs_ref[...]

    t_row = t_ref[...]
    t_col = column(t_row.astype(f32))
    owner_row = t_row >> 6
    owner_col = t_col.astype(i32) >> 6
    earlier = (owner_col == owner_row) & (iota((BLOCKS, BLOCKS), 0) < iota((BLOCKS, BLOCKS), 1))
    rank = jnp.sum(jnp.where(earlier, 1.0, 0.0), axis=0, keepdims=True).astype(i32)
    place = owner_row * CAP + rank
    pick = jnp.where(iota((nm * CAP, BLOCKS), 0) == place, 1.0, 0.0)
    qmat[...] = pick.astype(bf16)
    slot_row = ((t_row & (OWNED - 1)) + 1).astype(f32)
    slot_of = jnp.sum(pick * slot_row, axis=1, keepdims=True)
    slots[...] = jnp.broadcast_to(slot_of, (nm * CAP, CELLS)).reshape(nm, CAP, CELLS)

    def along_x(i, k):
        z = (mz + far_first(nz - 1 - i, nz)) % nz
        owner = z * NX + mx
        return remote(
            table_rows(owner), table_rows(owner), fan_send.at[i, k], ag_recv.at[owner],
            mesh=mz * NX + (mx + far_first(k, NX)) % NX,
        )

    def arrived(owner):
        return remote(table_rows(owner), table_rows(owner), ag_send.at[0], ag_recv.at[owner], mesh=right)

    own_table.wait()

    @pl.loop(0, nz)
    def _(i):
        z = (mz + far_first(nz - 1 - i, nz)) % nz

        @pl.when(i > 0)
        def _():
            arrived(z * NX + mx).wait_recv()

        @pl.loop(0, NX - 1)
        def _(k):
            along_x(i, k).start()

    def tell(i):
        m = mesh_at(i)
        return remote(slots.at[m], slots_in.at[me], sl_send.at[m], sl_recv.at[me], mesh=m)

    @pl.loop(0, nm - 1)
    def _(i):
        tell(i).start()

    for c in smalls:
        c.wait_recv()
    near_l, near_r = tn[0], tn[1]
    index = jnp.concatenate([near_l, t_row, near_r] + [t_row] * 5, axis=0)
    index_v[...] = (index >> 6) * half_rows + (index & (half_rows - 1))
    to_scalars = pltpu.make_async_copy(index_v, index_s, index_sem)
    to_scalars.start()

    mine_row = jnp.where(((t_row >> 5) & 1) == core, 1.0, 0.0)
    mine_l = jnp.where(((near_l >> 5) & 1) == core, 1.0, 0.0)
    mine_r = jnp.where(((near_r >> 5) & 1) == core, 1.0, 0.0)
    wide = (HALO, BLOCKS)
    col_l = jnp.sum(jnp.where(iota(wide, 0) + BLOCKS - HALO == iota(wide, 1), mine_l, 0.0), axis=1, keepdims=True)
    col_r = jnp.sum(jnp.where(iota(wide, 0) == iota(wide, 1), mine_r, 0.0), axis=1, keepdims=True)
    choose[0:HALO, :] = jnp.broadcast_to(col_l, (HALO, CELLS))
    choose[HALO:HALO + BLOCKS, :] = jnp.broadcast_to(column(mine_row), (BLOCKS, CELLS))
    choose[HALO + BLOCKS:, :] = jnp.broadcast_to(col_r, (HALO, CELLS))

    obs_swap.wait_recv()
    for side in range(2):
        for p in range(2):
            remote(obs_ref, obs_near.at[side, p], halo_send.at[side, p, 4], halo_recv.at[side, p, 4], comp=other).wait_recv()

    odd = iota((8, CELLS), 0) % 2

    def receivers(cells, base, obs_at):
        block = (cells >> 7) + base - HALF * odd
        lane = jnp.where(iota((CELLS, CELLS), 0) == (cells & (CELLS - 1)), 1.0, 0.0).astype(bf16)
        values = []
        for p in range(2):
            rows = [obs_at[p, pl.ds(4 * core + s, 1), :] for s in range(4)]
            values.append(jnp.concatenate([rows[r // 2] for r in range(8)], axis=0))
        return block, lane, values

    def scatter(block, lane, values, i):
        at = jnp.tile(block, (8, 1)) == 8 * i + (iota((64, CELLS), 0) >> 3)
        twice = jnp.concatenate([lane, lane], axis=1)
        res = []
        for v in values:
            hi, lo = two(jnp.where(at, jnp.tile(v, (8, 1)), 0.0))
            res.append(dot_t(jnp.concatenate([hi, lo], axis=1), twice))
        return res, dot_t(jnp.where(at, 1.0, 0.0).astype(bf16), lane)

    here = receivers(rcv_ref[...], HALO, obs_own)

    @pl.loop(0, HALF // 8)
    def _(i):
        res, cnt = scatter(*here, i)
        rows = pl.ds(pl.multiple_of(64 * i, 64), 64)
        heard[0, rows, :] = res[0]
        heard[1, rows, :] = res[1]
        count[rows, :] = cnt

    for side, (base, i) in enumerate(((HALO - BLOCKS, 0), (HALO + BLOCKS, HALF // 8 - 1))):
        res, cnt = scatter(*receivers(rn[side], base, obs_near.at[side]), i)
        rows = slice(64 * i, 64 * i + 64)
        heard[0, rows, :] += res[0]
        heard[1, rows, :] += res[1]
        count[rows, :] += cnt

    @pl.loop(0, 4)
    def _(s):
        own_copy(s).wait()
        exchange(s).wait_recv()

    @pl.loop(0, 8)
    def _(k):
        for side in range(2):
            remote(
                src_ref.at[0, pl.ds(0, HALO), :], stage_rows(k // 4, k % 4, 0 if side == 0 else STAGE - HALO, HALO),
                halo_send.at[side, k // 4, k % 4], halo_recv.at[side, k // 4, k % 4], comp=other,
            ).wait_recv()

    even_rows = iota((64, CELLS), 0) % 2 == 0
    keep_l = jnp.where(even_rows & (me == 0), 0.0, 1.0)
    keep_r = jnp.where(jnp.logical_not(even_rows) & (me == nm - 1), 0.0, 1.0)

    def keep(i):
        return jnp.where(i == 0, keep_l, jnp.where(i == HALF // 8 - 1, keep_r, 1.0))

    def put(b, p, i, x):
        x_buf[b, p, pl.ds(pl.multiple_of(8 + 64 * i, 8), 64), :] = x
        hi, lo = two(x)
        rows = pl.ds(pl.multiple_of(p * ROWS + 64 * i, 64), 64)
        lhs[rows, 0:CELLS] = hi
        lhs[rows, CELLS:] = lo

    def seams(b):
        top = iota((8, CELLS), 0) % 2 == 0
        for p in range(2):
            end = x_buf[b, p, ROWS:ROWS + 8, :]
            start = x_buf[b, p, 8:16, :]
            x_buf[b, p, 0:8, :] = jnp.where(top, 0.0, pltpu.roll(end, 1, axis=0))
            x_buf[b, p, ROWS + 8:ROWS + 16, :] = jnp.where(top, pltpu.roll(start, 7, axis=0), 0.0)

    @pl.loop(0, HALF // 8)
    def _(i):
        mask = keep(i)
        for p in range(2):
            x = jnp.concatenate(
                [stage[pl.ds(p * (4 * STAGE) + 8 * i + j, 8, stride=HALF), :] for j in range(8)], axis=0
            )
            x = x * dinv * mask
            q[0, p, pl.ds(pl.multiple_of(64 * i, 64), 64), :] = x
            put(0, p, i, x)

    seams(0)

    @pl.loop(0, nz)
    def _(i):
        z = (mz + far_first(i, nz)) % nz

        @pl.loop(0, NX - 1)
        def _(k):
            arrived(z * NX + (mx + far_first(k, NX)) % NX).wait_recv()

    to_scalars.wait()

    def pick_rows(first, source, lane):
        picked[pl.ds(first, 8), :] = jnp.concatenate(
            [table[pl.ds(index_s[source, lane + j], 1), :] for j in range(8)], axis=0
        )

    pick_rows(0, 0, BLOCKS - HALO)
    pick_rows(HALO + BLOCKS, 2, 0)

    @pl.loop(0, BLOCKS // 8)
    def _(i):
        pick_rows(pl.multiple_of(HALO + 8 * i, 8), 1, 8 * i)

    swap = remote(picked, theirs, pick_send.at[0], pick_recv.at[0], comp=other)
    swap.start()
    swap.wait_recv()
    sigma = OMEGA * jnp.exp(jnp.where(choose[...] > 0.5, picked[...], theirs[...]))
    wsig[...] = sigma

    @pl.loop(0, HALF // 8)
    def _(i):
        mask = keep(i)
        rows = []
        for j in range(8):
            a = jnp.broadcast_to(wsig[pl.ds(8 * i + j, 1), :], (8, CELLS))
            b = jnp.broadcast_to(wsig[pl.ds(HALF + 8 * i + j, 1), :], (8, CELLS))
            rows.append(jnp.where(odd == 0, a, b))
        cross[pl.ds(pl.multiple_of(64 * i, 64), 64), :] = jnp.concatenate(rows, axis=0) * dinv * mask

    lane_row = iota((1, CELLS), 1)
    at_first = jnp.where(lane_row == 0, CHAIN * dinv, 0.0)
    at_last = jnp.where(lane_row == CELLS - 1, CHAIN * dinv, 0.0)

    def sweep(base, qk, sign, weights, step):
        old, new = base + step % 2, base + (step + 1) % 2
        mm[...] = dot(lhs[...], weights[...])

        @pl.loop(0, HALF // 8, unroll=True)
        def _(i):
            mask = keep(i)
            rows = pl.ds(pl.multiple_of(64 * i, 64), 64)
            turn = cross[rows, :]
            for p in range(2):
                prod = pl.ds(pl.multiple_of(p * ROWS + 64 * i, 64), 64)
                before = x_buf[old, p, pl.ds(pl.multiple_of(64 * i, 8), 64), :]
                after = x_buf[old, p, pl.ds(pl.multiple_of(64 * i + 16, 8), 64), :]
                across = x_buf[old, 1 - p, pl.ds(pl.multiple_of(64 * i + 8, 8), 64), :]
                x = q[qk, p, rows, :] + (mm[prod, 0:CELLS] + mm[prod, CELLS:])
                x = x + at_first * pltpu.roll(before, 1, axis=1) + at_last * pltpu.roll(after, CELLS - 1, axis=1)
                both = turn * across
                x = x + both if (sign > 0) == (p == 0) else x - both
                put(new, p, i, x * mask)

        seams(new)

    @pl.loop(0, ITERS - 1)
    def _(step):
        sweep(0, 0, 1, wf, step)

    fin = (ITERS - 1) % 2

    @pl.loop(0, HALF // 8)
    def _(i):
        mask = keep(i) * dinv
        rows = pl.ds(pl.multiple_of(64 * i, 64), 64)
        for p in range(2):
            field = x_buf[fin, p, pl.ds(pl.multiple_of(8 + 64 * i, 8), 64), :]
            x = mask * (count[rows, :] * field - heard[p, rows, :])
            q[1, p, rows, :] = x
            put(2, p, i, x)

    seams(2)

    @pl.loop(0, ITERS - 1)
    def _(step):
        sweep(2, 1, -1, wa, step)

    @pl.loop(0, HALF // 8)
    def _(i):
        rows = pl.ds(pl.multiple_of(8 + 64 * i, 8), 64)
        psum_buf[pl.ds(pl.multiple_of(64 * i, 64), 64), :] = (
            x_buf[2 + fin, 0, rows, :] * x_buf[fin, 1, rows, :]
            - x_buf[2 + fin, 1, rows, :] * x_buf[fin, 0, rows, :]
        )

    @pl.loop(0, BLOCKS // 16)
    def _(i):
        for h in range(2):
            first = 8 * (8 * i + (HALO if h == 0 else 0)) + h
            acc = psum_buf[pl.ds(first, 8, stride=8), :]
            for s in range(1, 4):
                acc = acc + psum_buf[pl.ds(first + 2 * s, 8, stride=8), :]
            at = 8 * i + (HALF - HALO) * h
            part[pl.ds(pl.multiple_of(at, 8), 8), :] = acc * wsig[pl.ds(pl.multiple_of(HALO + at, 8), 8), :]

    hi, mid, lo = three(part[...])
    sel = qmat[...]
    packed = dot(sel, hi) + dot(sel, mid) + dot(sel, lo)
    pack[...] = packed.reshape(nm, CAP, CELLS)

    def give(i):
        m = mesh_at(i)
        return remote(pack.at[m], pack_in.at[me], gp_send.at[m], gp_recv.at[me], mesh=m)

    @pl.loop(0, nm - 1)
    def _(i):
        give(i).start()

    pack_in[me] = pack[me]
    slots_in[me] = slots[me]

    @pl.loop(0, nm - 1)
    def _(i):
        m = mesh_at(i)
        remote(slots.at[m], slots_in.at[m], sl_send.at[m], sl_recv.at[m], mesh=m).wait_recv()

    slot_in = slots_in[...].reshape(nm * CAP, CELLS)
    hit = jnp.where(slot_in == (iota((nm * CAP, CELLS), 1) + 1).astype(f32), 1.0, 0.0)
    hits[...] = hit.T.astype(bf16)

    @pl.loop(0, nm - 1)
    def _(i):
        m = mesh_at(i)
        remote(pack.at[m], pack_in.at[m], gp_send.at[m], gp_recv.at[m], mesh=m).wait_recv()

    hi, mid, lo = three(pack_in[...].reshape(nm * CAP, CELLS))
    sel = hits[0:OWNED, :]
    grad[...] = dot(sel, hi) + dot(sel, mid) + dot(sel, lo)

    def half_of(ref, c):
        return ref.at[pl.ds(pl.multiple_of(c * half_rows, 8), half_rows), :]

    cores = remote(half_of(grad, other), grad_in, gr_send.at[0], gr_recv.at[0], comp=other)
    cores.start()
    cores.wait_recv()
    line[grp] = grad[pl.ds(pl.multiple_of(core * half_rows, 8), half_rows), :] + grad_in[...]

    def over_y(d):
        return remote(line.at[grp], line.at[grp], ln_send.at[d], ln_recv.at[grp], group=(grp + far_first(d, ng)) % ng)

    @pl.loop(0, ng - 1)
    def _(d):
        over_y(d).start()

    @pl.loop(0, ng - 1)
    def _(d):
        g = (grp + far_first(d, ng)) % ng
        remote(line.at[g], line.at[g], ln_send.at[d], ln_recv.at[g], group=g).wait_recv()

    summed = line[0]
    for g in range(1, ng):
        summed = summed + line[g]
    total[...] = summed
    back = remote(total, total_in, to_send.at[0], to_recv.at[0], comp=other)
    back.start()
    out_ref[pl.ds(pl.multiple_of(core * half_rows, 8), half_rows), :] = summed
    back.wait_recv()
    out_ref[pl.ds(pl.multiple_of(other * half_rows, 8), half_rows), :] = total_in[...]

    @pl.loop(0, nz - 1)
    def _(i):
        along_z(i).wait_send()

    for c in smalls:
        c.wait_send()

    @pl.loop(0, 4)
    def _(s):
        exchange(s).wait_send()

    @pl.loop(0, 8)
    def _(k):
        halo(0, k // 4, k % 4).wait_send()
        halo(1, k // 4, k % 4).wait_send()

    @pl.loop(0, 2)
    def _(c):
        obs_to(0, c).wait_send()
        obs_to(1, c).wait_send()

    obs_swap.wait_send()

    @pl.loop(0, nz)
    def _(i):
        @pl.loop(0, NX - 1)
        def _(k):
            along_x(i, k).wait_send()

    swap.wait_send()

    @pl.loop(0, nm - 1)
    def _(i):
        tell(i).wait_send()
        give(i).wait_send()

    cores.wait_send()

    @pl.loop(0, ng - 1)
    def _(d):
        over_y(d).wait_send()

    back.wait_send()


def local(log_sigma, block_owner, block_slot, coupling, sources, rcv_cell, observed):
    nm, ng = lax.axis_size("mesh"), lax.axis_size("group")
    targets = block_owner.reshape(1, BLOCKS) * OWNED + block_slot
    vmem, hbm, dma = pltpu.VMEM, pl.BlockSpec(memory_space=pl.ANY), pltpu.SemaphoreType.DMA
    inside = pl.BlockSpec(memory_space=pltpu.VMEM)
    nz = nm // NX
    return pl.pallas_call(
        functools.partial(kernel, ng, nm),
        out_shape=jax.ShapeDtypeStruct((OWNED, CELLS), f32),
        in_specs=[inside] * 4 + [hbm] * 2,
        out_specs=inside,
        scratch_shapes=[
            vmem((8 * STAGE, CELLS), f32),
            vmem((nm * OWNED // 2, CELLS), f32),
            vmem((2, 1, BLOCKS), i32),
            vmem((2, 1, BLOCKS), i32),
            vmem((2, S, CELLS), f32),
            vmem((2, 2, S, CELLS), f32),
            vmem((8, BLOCKS), i32),
            pltpu.SMEM((8, BLOCKS), i32),
            vmem((STAGE, CELLS), f32),
            vmem((STAGE, CELLS), f32),
            vmem((STAGE, CELLS), f32),
            vmem((4, 2, ROWS + 16, CELLS), f32),
            vmem((2 * ROWS, 2 * CELLS), bf16),
            vmem((2 * ROWS, 2 * CELLS), f32),
            vmem((2, 2, ROWS, CELLS), f32),
            vmem((ROWS, CELLS), f32),
            vmem((STAGE, CELLS), f32),
            vmem((CELLS, nm * CAP), bf16),
            vmem((2, ROWS, CELLS), f32),
            vmem((ROWS, CELLS), f32),
            vmem((2 * CELLS, 2 * CELLS), bf16),
            vmem((2 * CELLS, 2 * CELLS), bf16),
            vmem((nm * CAP, BLOCKS), bf16),
            vmem((ROWS, CELLS), f32),
            vmem((BLOCKS, CELLS), f32),
            vmem((nm, CAP, CELLS), f32),
            vmem((nm, CAP, CELLS), f32),
            vmem((nm, CAP, CELLS), f32),
            vmem((nm, CAP, CELLS), f32),
            vmem((OWNED, CELLS), f32),
            vmem((OWNED // 2, CELLS), f32),
            vmem((ng, OWNED // 2, CELLS), f32),
            vmem((OWNED // 2, CELLS), f32),
            vmem((OWNED // 2, CELLS), f32),
            dma((5,)),
            dma((5,)), dma((5,)),
            dma((2, 2, 5)), dma((2, 2, 5)),
            dma((2, 2)), dma((2, 2)),
            dma((nz,)), dma((nm,)), dma((nz, NX)),
            dma((1,)), dma((1,)),
            dma((nm,)), dma((nm,)),
            dma((nm,)), dma((nm,)),
            dma((1,)), dma((1,)),
            dma((ng,)), dma((ng,)),
            dma((1,)), dma((1,)),
            dma(()),
        ],
        compiler_params=pltpu.CompilerParams(collective_id=0, has_side_effects=True),
    )(
        targets, rcv_cell, observed.reshape(S, CELLS), coupling, log_sigma, sources.reshape(S, BLOCKS, CELLS)
    )


def solution(mesh):
    in_specs = (
        P("mesh", None),
        P("group", "mesh", None),
        P("group", "mesh"),
        P(),
        P("group", "comp", None, "mesh", None),
        P("group", "mesh"),
        P("group", "comp", None, "mesh"),
    )
    return jax.shard_map(local, mesh=mesh, in_specs=in_specs, out_specs=P("mesh", None), check_vma=False)
```

```python
import functools

import jax
import jax.numpy as jnp
from jax import lax
from jax.experimental import pallas as pl
from jax.experimental.pallas import tpu as pltpu
from jax.sharding import PartitionSpec as P

CELLS = 128
S = 8
ITERS = 6
CAP = 8
NX = 4
BLOCKS = 128
HALO = 8
HALF = (BLOCKS + 2 * HALO) // 2
ROWS = HALF * 8
STAGE = BLOCKS + 2 * HALO
OWNED = 64
GROUP = 9
OMEGA = 0.8
CHAIN = 1.0

f32, bf16, i32 = jnp.float32, jnp.bfloat16, jnp.int32
NT = (((1,), (1,)), ((), ()))


def iota(shape, dim):
    return lax.broadcasted_iota(i32, shape, dim)


def two(x):
    hi = x.astype(bf16)
    return hi, (x - hi.astype(f32)).astype(bf16)


def three(x):
    hi = x.astype(bf16)
    rest = x - hi.astype(f32)
    mid = rest.astype(bf16)
    return hi, mid, (rest - mid.astype(f32)).astype(bf16)


def dot(a, b):
    return jnp.dot(a, b, preferred_element_type=f32)


def dot_t(a, b):
    return lax.dot_general(a, b, NT, preferred_element_type=f32)


def column(row):
    n = row.shape[1]
    return jnp.sum(jnp.where(iota((n, n), 0) == iota((n, n), 1), row, 0.0), axis=1, keepdims=True)


def kernel(
    ng, nm, own_ref, slot_ref, rcv_ref, obs_ref, cpl_ref, ls_ref, src_ref, out_ref,
    stage, table, near, obs_own, obs_near, index_v, index_s, picked, theirs, choose,
    fwd_a, fwd_b, adj_a, adj_b, lhs_hi, lhs_lo, q, cross, wsig, hits, heard, count, wf, wa, qmat, psum_buf, part,
    slots, slots_in, pack, pack_in, grad, grad_in, line, total, total_in,
    local_sem, ex_send, ex_recv, halo_send, halo_recv, obs_send, obs_recv, small_send, small_recv,
    ag_send, ag_recv, fan_send, fan_recv, pick_send, pick_recv, sl_send, sl_recv, gp_send, gp_recv,
    gr_send, gr_recv, ln_send, ln_recv, to_send, to_recv, index_sem,
):
    me = lax.axis_index("mesh")
    core = lax.axis_index("comp")
    grp = lax.axis_index("group")
    other = 1 - core
    nz = nm // NX
    mz, mx = lax.div(me, NX), lax.rem(me, NX)
    z_at = [lax.rem(mz + d, nz) * NX for d in range(nz)]
    x_at = [lax.rem(mx + d, NX) for d in range(NX)]
    g_at = [lax.rem(grp + d, ng) for d in range(ng)]
    right, left = lax.rem(me + 1, nm), lax.rem(me + nm - 1, nm)

    def ring(d, n):
        return min(d, n - d)

    far_z, far_x, far_g = (sorted(range(1, n), key=lambda d: -ring(d, n)) for n in (nz, NX, ng))
    far = sorted(
        [(z, x) for z in range(nz) for x in range(NX) if z or x], key=lambda d: -ring(d[0], nz) - ring(d[1], NX)
    )

    def remote(src, dst, ssem, rsem, g=None, m=None, c=None):
        where = (grp if g is None else g, me if m is None else m, core if c is None else c)
        return pltpu.make_async_remote_copy(
            src_ref=src, dst_ref=dst, send_sem=ssem, recv_sem=rsem,
            device_id=where, device_id_type=pl.DeviceIdType.MESH,
        )

    def bytes_of(ref, ssem, rsem):
        return remote(ref, ref, ssem, rsem, c=other)

    barrier = pltpu.get_barrier_semaphore()

    def greet(g=None, m=None, c=None):
        where = (grp if g is None else g, me if m is None else m, core if c is None else c)
        pl.semaphore_signal(barrier, inc=1, device_id=where, device_id_type=pl.DeviceIdType.MESH)

    for z, x in far:
        greet(m=z_at[z] + x_at[x])
    for d in far_g:
        greet(g=g_at[d])
    greet(m=left, c=other)
    greet(m=right, c=other)
    greet(c=other)

    half_rows = OWNED // 2
    own_half = pl.ds(pl.multiple_of(core * half_rows, 8), half_rows)

    def table_rows(owner):
        return table.at[pl.ds(pl.multiple_of(owner * half_rows, 8), half_rows), :]

    def stage_rows(p, s, first, n):
        return stage.at[pl.ds(pl.multiple_of(p * (4 * STAGE) + s * STAGE + first, 8), n), :]

    own_table = pltpu.make_async_copy(ls_ref.at[own_half, :], table_rows(me), local_sem.at[1])
    own_table.start()
    own_src = [
        pltpu.make_async_copy(src_ref.at[4 * core + s], stage_rows(core, s, HALO, BLOCKS), local_sem.at[s + 2])
        for s in range(4)
    ]
    for c in own_src:
        c.start()

    pl.semaphore_wait(barrier, nm - 1 + ng - 1 + 3)

    for z in far_z:
        remote(ls_ref.at[own_half, :], table_rows(me), ag_send.at[0], ag_recv.at[mz], m=z_at[z] + mx).start()

    for side, m in ((0, right), (1, left)):
        for k, ref in enumerate((own_ref, slot_ref, rcv_ref)):
            remote(ref, near.at[side, k], small_send.at[0], small_recv.at[0], m=m).start()
    for s in range(4):
        remote(
            src_ref.at[4 * other + s], stage_rows(core, s, HALO, BLOCKS), ex_send.at[0], ex_recv.at[0], c=other
        ).start()
    obs_swap = remote(obs_ref, obs_own.at[core], ex_send.at[1], ex_recv.at[1], c=other)
    obs_swap.start()
    for side, m, first, into in ((0, right, BLOCKS - HALO, 0), (1, left, 0, STAGE - HALO)):
        for c in range(2):
            for s in range(4):
                remote(
                    src_ref.at[4 * c + s, pl.ds(first, HALO), :], stage_rows(core, s, into, HALO),
                    halo_send.at[0], halo_recv.at[0], m=m, c=c,
                ).start()
            remote(obs_ref, obs_near.at[side, core], obs_send.at[0], obs_recv.at[0], m=m, c=c).start()
    obs_own[core] = obs_ref[...]

    eye = iota((CELLS, CELLS), 0) == iota((CELLS, CELLS), 1)
    beside = jnp.abs(iota((CELLS, CELLS), 0) - iota((CELLS, CELLS), 1)) == 1
    cpl = cpl_ref[...]
    dinv = 1.0 / jnp.sum(jnp.where(eye, cpl, 0.0), axis=0, keepdims=True)
    for m, w in ((cpl.T, wf), (cpl, wa)):
        scaled = -dinv * (jnp.where(eye, 0.0, m) - jnp.where(beside, CHAIN, 0.0))
        hi, lo = two(scaled)
        w[0:CELLS, 0:CELLS] = hi
        w[0:CELLS, CELLS:] = lo
        w[CELLS:, 0:CELLS] = hi
        w[CELLS:, CELLS:] = lo

    owner_row = own_ref[...]
    slot_row = slot_ref[...]
    owner_col = column(owner_row.astype(f32)).astype(i32)
    earlier = (owner_col == owner_row) & (iota((BLOCKS, BLOCKS), 0) < iota((BLOCKS, BLOCKS), 1))
    rank = jnp.sum(jnp.where(earlier, 1.0, 0.0), axis=0, keepdims=True).astype(i32)
    place = owner_row * CAP + rank
    pick = jnp.where(iota((nm * CAP, BLOCKS), 0) == place, 1.0, 0.0)
    qmat[...] = pick.astype(bf16)
    slot_of = jnp.sum(pick * (slot_row + 1).astype(f32), axis=1, keepdims=True)
    slots[...] = jnp.broadcast_to(slot_of, (nm * CAP, CELLS)).reshape(nm, CAP, CELLS)

    own_table.wait()
    for z in [0] + far_z[::-1]:
        owner = z_at[z] + mx
        if z:
            remote(
                table_rows(owner), table_rows(owner), ag_send.at[0], ag_recv.at[lax.div(z_at[z], NX)], c=other
            ).wait_recv()
        for x in far_x:
            remote(
                table_rows(owner), table_rows(owner), fan_send.at[0], fan_recv.at[0], m=z_at[0] + x_at[x]
            ).start()

    for z, x in far:
        m = z_at[z] + x_at[x]
        remote(slots.at[m], slots_in.at[me], sl_send.at[0], sl_recv.at[0], m=m).start()

    bytes_of(near, small_send.at[0], small_recv.at[0]).wait_recv()
    own3 = jnp.concatenate([near[0, 0], owner_row, near[1, 0]] + [owner_row] * 5, axis=0)
    slot3 = jnp.concatenate([near[0, 1], slot_row, near[1, 1]] + [slot_row] * 5, axis=0)
    index_v[...] = own3 * half_rows + (slot3 & (half_rows - 1))
    to_scalars = pltpu.make_async_copy(index_v, index_s, index_sem)
    to_scalars.start()

    mine = jnp.where((slot3 >> 5) == core, 1.0, 0.0)
    wide = (HALO, BLOCKS)
    col_l = jnp.sum(jnp.where(iota(wide, 0) + BLOCKS - HALO == iota(wide, 1), mine[0:1], 0.0), axis=1, keepdims=True)
    col_r = jnp.sum(jnp.where(iota(wide, 0) == iota(wide, 1), mine[2:3], 0.0), axis=1, keepdims=True)
    choose[0:HALO, :] = jnp.broadcast_to(col_l, (HALO, CELLS))
    choose[HALO:HALO + BLOCKS, :] = jnp.broadcast_to(column(mine[1:2]), (BLOCKS, CELLS))
    choose[HALO + BLOCKS:, :] = jnp.broadcast_to(col_r, (HALO, CELLS))

    obs_swap.wait_recv()
    bytes_of(obs_near, obs_send.at[0], obs_recv.at[0]).wait_recv()
    odd = iota((8, CELLS), 0) % 2

    def receivers(cells, base, obs_at):
        block = (cells >> 7) + base - HALF * odd
        lane = jnp.where(iota((CELLS, CELLS), 0) == (cells & (CELLS - 1)), 1.0, 0.0).astype(bf16)
        values = []
        for p in range(2):
            rows = [obs_at[p, pl.ds(4 * core + s, 1), :] for s in range(4)]
            values.append(jnp.concatenate([rows[r // 2] for r in range(8)], axis=0))
        return block, lane, values

    def scatter(block, lane, values, i):
        at = jnp.tile(block, (8, 1)) == 8 * i + (iota((64, CELLS), 0) >> 3)
        twice = jnp.concatenate([lane, lane], axis=1)
        res = []
        for v in values:
            hi, lo = two(jnp.where(at, jnp.tile(v, (8, 1)), 0.0))
            res.append(dot_t(jnp.concatenate([hi, lo], axis=1), twice))
        return res, dot_t(jnp.where(at, 1.0, 0.0).astype(bf16), lane)

    here = receivers(rcv_ref[...], HALO, obs_own)

    @pl.loop(0, HALF // 8)
    def _(i):
        res, cnt = scatter(*here, i)
        rows = pl.ds(pl.multiple_of(64 * i, 64), 64)
        heard[0, rows, :] = res[0]
        heard[1, rows, :] = res[1]
        count[rows, :] = cnt

    last = HALF // 8 - 1
    for side, base, i in ((0, HALO - BLOCKS, 0), (1, HALO + BLOCKS, last)):
        res, cnt = scatter(*receivers(near[side, 2], base, obs_near.at[side]), i)
        rows = slice(64 * i, 64 * i + 64)
        heard[0, rows, :] += res[0]
        heard[1, rows, :] += res[1]
        count[rows, :] += cnt

    for c in own_src:
        c.wait()
    bytes_of(stage.at[0:4 * BLOCKS, :], ex_send.at[0], ex_recv.at[0]).wait_recv()
    bytes_of(stage.at[0:16 * HALO, :], halo_send.at[0], halo_recv.at[0]).wait_recv()

    even_rows = iota((64, CELLS), 0) % 2 == 0
    keep_l = jnp.where(even_rows & (me == 0), 0.0, 1.0)
    keep_r = jnp.where(jnp.logical_not(even_rows) & (me == nm - 1), 0.0, 1.0)

    def kept(i, x):
        if isinstance(i, int):
            return x * keep_l if i == 0 else x * keep_r if i == last else x
        return x * jnp.where(i == 0, keep_l, jnp.where(i == last, keep_r, 1.0))

    def at64(i, first=0):
        return slice(first + 64 * i, first + 64 * i + 64) if isinstance(i, int) else pl.ds(
            pl.multiple_of(first + 64 * i, 8), 64)

    def put(b, p, i, x):
        b[p, at64(i, 8), :] = x
        hi, lo = two(x)
        lhs_hi[at64(2 * i + p), :] = hi
        lhs_lo[at64(2 * i + p), :] = lo

    def seams(b):
        top = iota((8, CELLS), 0) % 2 == 0
        for p in range(2):
            end = b[p, ROWS:ROWS + 8, :]
            start = b[p, 8:16, :]
            b[p, 0:8, :] = jnp.where(top, 0.0, pltpu.roll(end, 1, axis=0))
            b[p, ROWS + 8:ROWS + 16, :] = jnp.where(top, pltpu.roll(start, 7, axis=0), 0.0)

    @pl.loop(0, HALF // 8)
    def _(i):
        for p in range(2):
            x = jnp.concatenate(
                [stage[pl.ds(p * (4 * STAGE) + 8 * i + j, 8, stride=HALF), :] for j in range(8)], axis=0
            )
            x = kept(i, x * dinv)
            q[0, p, at64(i), :] = x
            put(fwd_a, p, i, x)

    seams(fwd_a)

    bytes_of(table.at[0:nz * (NX - 1) * half_rows, :], fan_send.at[0], fan_recv.at[0]).wait_recv()
    to_scalars.wait()

    def pick_rows(first, source, lane):
        picked[pl.ds(first, 8), :] = jnp.concatenate(
            [table[pl.ds(index_s[source, lane + j], 1), :] for j in range(8)], axis=0
        )

    pick_rows(0, 0, BLOCKS - HALO)
    pick_rows(HALO + BLOCKS, 2, 0)

    @pl.loop(0, BLOCKS // 8)
    def _(i):
        pick_rows(pl.multiple_of(HALO + 8 * i, 8), 1, 8 * i)

    swap = remote(picked, theirs, pick_send.at[0], pick_recv.at[0], c=other)
    swap.start()
    swap.wait_recv()
    wsig[...] = OMEGA * jnp.exp(jnp.where(choose[...] > 0.5, picked[...], theirs[...]))

    @pl.loop(0, HALF // 8)
    def _(i):
        rows = []
        for j in range(8):
            a = jnp.broadcast_to(wsig[pl.ds(8 * i + j, 1), :], (8, CELLS))
            b = jnp.broadcast_to(wsig[pl.ds(HALF + 8 * i + j, 1), :], (8, CELLS))
            rows.append(jnp.where(odd == 0, a, b))
        cross[at64(i), :] = kept(i, jnp.concatenate(rows, axis=0) * dinv)

    lane_row = iota((1, CELLS), 1)
    at_first = jnp.where(lane_row == 0, CHAIN * dinv, 0.0)
    at_last = jnp.where(lane_row == CELLS - 1, CHAIN * dinv, 0.0)

    def sweep(old, new, qk, sign, weights):
        for first in range(0, HALF // 8, GROUP):
            rows = slice(128 * first, 128 * (first + GROUP))
            prod = dot(jnp.concatenate([lhs_hi[rows, :], lhs_lo[rows, :]], axis=1), weights[...])
            prod = prod[:, 0:CELLS] + prod[:, CELLS:]
            for i in range(first, first + GROUP):
                turn = cross[at64(i), :]
                for p in range(2):
                    k = 2 * (i - first) + p
                    before = old[p, at64(i), :]
                    after = old[p, at64(i, 16), :]
                    both = turn * old[1 - p, at64(i, 8), :]
                    x = q[qk, p, at64(i), :] + prod[64 * k:64 * k + 64, :]
                    x = x + at_first * pltpu.roll(before, 1, axis=1) + at_last * pltpu.roll(after, CELLS - 1, axis=1)
                    x = x + both if (sign > 0) == (p == 0) else x - both
                    put(new, p, i, kept(i, x))
        seams(new)

    def sweeps(a, b, *args):
        sweep(a, b, *args)

        @pl.loop(0, ITERS // 2 - 1)
        def _(k):
            sweep(b, a, *args)
            sweep(a, b, *args)

    sweeps(fwd_a, fwd_b, 0, 1, wf)

    @pl.loop(0, HALF // 8)
    def _(i):
        for p in range(2):
            x = count[at64(i), :] * fwd_b[p, at64(i, 8), :] - heard[p, at64(i), :]
            x = kept(i, x * dinv)
            q[1, p, at64(i), :] = x
            put(adj_a, p, i, x)

    seams(adj_a)

    sweeps(adj_a, adj_b, 1, -1, wa)

    for i in range(HALF // 8):
        psum_buf[at64(i), :] = (
            adj_b[0, at64(i, 8), :] * fwd_b[1, at64(i, 8), :]
            - adj_b[1, at64(i, 8), :] * fwd_b[0, at64(i, 8), :]
        )

    for i in range(BLOCKS // 16):
        for h in range(2):
            first = 8 * (8 * i + (HALO if h == 0 else 0)) + h
            acc = psum_buf[pl.ds(first, 8, stride=8), :]
            for s in range(1, 4):
                acc = acc + psum_buf[pl.ds(first + 2 * s, 8, stride=8), :]
            at = 8 * i + (HALF - HALO) * h
            part[at:at + 8, :] = acc * wsig[HALO + at:HALO + at + 8, :]

    hi, mid, lo = three(part[...])
    sel = qmat[...]
    packed = dot(sel, hi) + dot(sel, mid) + dot(sel, lo)
    pack[...] = packed.reshape(nm, CAP, CELLS)

    for z, x in far:
        m = z_at[z] + x_at[x]
        remote(pack.at[m], pack_in.at[me], gp_send.at[0], gp_recv.at[0], m=m).start()

    pack_in[me] = pack[me]
    bytes_of(slots.at[0:nm - 1], sl_send.at[0], sl_recv.at[0]).wait_recv()
    slots_in[me] = slots[me]
    slot_in = slots_in[...].reshape(nm * CAP, CELLS)
    hit = jnp.where(slot_in == (iota((nm * CAP, CELLS), 1) + 1).astype(f32), 1.0, 0.0)
    hits[...] = hit.T.astype(bf16)

    bytes_of(table.at[0:(nz - 1) * half_rows, :], ag_send.at[0], ag_recv.at[0]).wait_send()
    bytes_of(near, small_send.at[0], small_recv.at[0]).wait_send()
    bytes_of(stage.at[0:4 * BLOCKS, :], ex_send.at[0], ex_recv.at[0]).wait_send()
    obs_swap.wait_send()
    bytes_of(stage.at[0:16 * HALO, :], halo_send.at[0], halo_recv.at[0]).wait_send()
    bytes_of(obs_near, obs_send.at[0], obs_recv.at[0]).wait_send()
    bytes_of(table.at[0:nz * (NX - 1) * half_rows, :], fan_send.at[0], fan_recv.at[0]).wait_send()
    swap.wait_send()
    bytes_of(slots.at[0:nm - 1], sl_send.at[0], sl_recv.at[0]).wait_send()

    bytes_of(pack.at[0:nm - 1], gp_send.at[0], gp_recv.at[0]).wait_recv()
    hi, mid, lo = three(pack_in[...].reshape(nm * CAP, CELLS))
    sel = hits[0:OWNED, :]
    grad[...] = dot(sel, hi) + dot(sel, mid) + dot(sel, lo)

    mine_half = pl.ds(pl.multiple_of(core * half_rows, 8), half_rows)
    their_half = pl.ds(pl.multiple_of(other * half_rows, 8), half_rows)
    cores = remote(grad.at[their_half, :], grad_in, gr_send.at[0], gr_recv.at[0], c=other)
    cores.start()
    cores.wait_recv()
    line[grp] = grad[mine_half, :] + grad_in[...]
    for d in far_g:
        remote(line.at[grp], line.at[grp], ln_send.at[0], ln_recv.at[0], g=g_at[d]).start()
    cores.wait_send()
    bytes_of(pack.at[0:nm - 1], gp_send.at[0], gp_recv.at[0]).wait_send()
    bytes_of(line.at[0:ng - 1], ln_send.at[0], ln_recv.at[0]).wait_recv()

    summed = line[0]
    for g in range(1, ng):
        summed = summed + line[g]
    total[...] = summed
    back = remote(total, total_in, to_send.at[0], to_recv.at[0], c=other)
    back.start()
    out_ref[mine_half, :] = summed
    bytes_of(line.at[0:ng - 1], ln_send.at[0], ln_recv.at[0]).wait_send()
    back.wait()
    out_ref[their_half, :] = total_in[...]


def local(log_sigma, block_owner, block_slot, coupling, sources, rcv_cell, observed):
    nm, ng = lax.axis_size("mesh"), lax.axis_size("group")
    vmem, hbm, dma = pltpu.VMEM, pl.BlockSpec(memory_space=pl.ANY), pltpu.SemaphoreType.DMA
    inside = pl.BlockSpec(memory_space=pltpu.VMEM)
    nz = nm // NX
    return pl.pallas_call(
        functools.partial(kernel, ng, nm),
        out_shape=jax.ShapeDtypeStruct((OWNED, CELLS), f32),
        in_specs=[inside] * 5 + [hbm] * 2,
        out_specs=inside,
        scratch_shapes=[
            vmem((8 * STAGE, CELLS), f32),
            vmem((nm * OWNED // 2, CELLS), f32),
            vmem((2, 3, 1, BLOCKS), i32),
            vmem((2, S, CELLS), f32),
            vmem((2, 2, S, CELLS), f32),
            vmem((8, BLOCKS), i32),
            pltpu.SMEM((8, BLOCKS), i32),
            vmem((STAGE, CELLS), f32),
            vmem((STAGE, CELLS), f32),
            vmem((STAGE, CELLS), f32),
            vmem((2, ROWS + 16, CELLS), f32),
            vmem((2, ROWS + 16, CELLS), f32),
            vmem((2, ROWS + 16, CELLS), f32),
            vmem((2, ROWS + 16, CELLS), f32),
            vmem((2 * ROWS, CELLS), bf16),
            vmem((2 * ROWS, CELLS), bf16),
            vmem((2, 2, ROWS, CELLS), f32),
            vmem((ROWS, CELLS), f32),
            vmem((STAGE, CELLS), f32),
            vmem((CELLS, nm * CAP), bf16),
            vmem((2, ROWS, CELLS), f32),
            vmem((ROWS, CELLS), f32),
            vmem((2 * CELLS, 2 * CELLS), bf16),
            vmem((2 * CELLS, 2 * CELLS), bf16),
            vmem((nm * CAP, BLOCKS), bf16),
            vmem((ROWS, CELLS), f32),
            vmem((BLOCKS, CELLS), f32),
            vmem((nm, CAP, CELLS), f32),
            vmem((nm, CAP, CELLS), f32),
            vmem((nm, CAP, CELLS), f32),
            vmem((nm, CAP, CELLS), f32),
            vmem((OWNED, CELLS), f32),
            vmem((OWNED // 2, CELLS), f32),
            vmem((ng, OWNED // 2, CELLS), f32),
            vmem((OWNED // 2, CELLS), f32),
            vmem((OWNED // 2, CELLS), f32),
            dma((6,)),
            dma((2,)), dma((2,)),
            dma((1,)), dma((1,)),
            dma((1,)), dma((1,)),
            dma((1,)), dma((1,)),
            dma((1,)), dma((nz,)),
            dma((1,)), dma((1,)),
            dma((1,)), dma((1,)),
            dma((1,)), dma((1,)),
            dma((1,)), dma((1,)),
            dma((1,)), dma((1,)),
            dma((1,)), dma((1,)),
            dma((1,)), dma((1,)),
            dma(()),
        ],
        compiler_params=pltpu.CompilerParams(collective_id=0, has_side_effects=True),
    )(
        block_owner.reshape(1, BLOCKS), block_slot, rcv_cell, observed.reshape(S, CELLS), coupling, log_sigma, sources.reshape(S, BLOCKS, CELLS)
    )


def solution(mesh):
    in_specs = (
        P("mesh", None),
        P("group", "mesh", None),
        P("group", "mesh"),
        P(),
        P("group", "comp", None, "mesh", None),
        P("group", "mesh"),
        P("group", "comp", None, "mesh"),
    )
    return jax.shard_map(local, mesh=mesh, in_specs=in_specs, out_specs=P("mesh", None), check_vma=False)
```

```python
import functools

import jax
import jax.numpy as jnp
from jax import lax
from jax.experimental import pallas as pl
from jax.experimental.pallas import tpu as pltpu
from jax.sharding import PartitionSpec as P

CELLS = 128
S = 8
ITERS = 6
CAP = 8
NX = 4
BLOCKS = 128
HALO = 8
HALF = (BLOCKS + 2 * HALO) // 2
ROWS = HALF * 8
STAGE = BLOCKS + 2 * HALO
OWNED = 64
GROUP = 9
OMEGA = 0.8
CHAIN = 1.0

f32, bf16, i32 = jnp.float32, jnp.bfloat16, jnp.int32
NT = (((1,), (1,)), ((), ()))


def iota(shape, dim):
    return lax.broadcasted_iota(i32, shape, dim)


def two(x):
    hi = x.astype(bf16)
    return hi, (x - hi.astype(f32)).astype(bf16)


def three(x):
    hi = x.astype(bf16)
    rest = x - hi.astype(f32)
    mid = rest.astype(bf16)
    return hi, mid, (rest - mid.astype(f32)).astype(bf16)


def dot(a, b):
    return jnp.dot(a, b, preferred_element_type=f32)


def dot_t(a, b):
    return lax.dot_general(a, b, NT, preferred_element_type=f32)


def column(row):
    n = row.shape[1]
    return jnp.sum(jnp.where(iota((n, n), 0) == iota((n, n), 1), row, 0.0), axis=1, keepdims=True)


def kernel(
    ng, nm, own_ref, slot_ref, rcv_ref, obs_ref, cpl_ref, ls_ref, src_ref, low_ref, high_ref,
    stage, table, near, self_v, cpl_v, obs_own, obs_near, index_v, index_s, picked, theirs, choose,
    fwd_a, fwd_b, adj_a, adj_b, lhs_hi, lhs_lo, q, cross, wsig, hits, heard, count, wf, wa, qmat, psum_buf, part,
    slots, slots_in, pack, pack_in, grad, grad_in, line, total, total_in,
    local_sem, ex_send, ex_recv, halo_send, halo_recv, obs_send, obs_recv, small_send, small_recv,
    ag_send, ag_recv, fan_send, fan_recv, pick_send, pick_recv, sl_send, sl_recv, gp_send, gp_recv,
    gr_send, gr_recv, ln_send, ln_recv, to_send, to_recv, index_sem,
):
    me = lax.axis_index("mesh")
    core = lax.axis_index("comp")
    grp = lax.axis_index("group")
    other = 1 - core
    nz = nm // NX
    mz, mx = lax.div(me, NX), lax.rem(me, NX)
    z_at = [lax.rem(mz + d, nz) * NX for d in range(nz)]
    x_at = [lax.rem(mx + d, NX) for d in range(NX)]
    g_at = [lax.rem(grp + d, ng) for d in range(ng)]
    right, left = lax.rem(me + 1, nm), lax.rem(me + nm - 1, nm)

    def ring(d, n):
        return min(d, n - d)

    far_z, far_x, far_g = (sorted(range(1, n), key=lambda d: -ring(d, n)) for n in (nz, NX, ng))
    far = sorted(
        [(z, x) for z in range(nz) for x in range(NX) if z or x], key=lambda d: -ring(d[0], nz) - ring(d[1], NX)
    )

    def remote(src, dst, ssem, rsem, g=None, m=None, c=None):
        where = (grp if g is None else g, me if m is None else m, core if c is None else c)
        return pltpu.make_async_remote_copy(
            src_ref=src, dst_ref=dst, send_sem=ssem, recv_sem=rsem,
            device_id=where, device_id_type=pl.DeviceIdType.MESH,
        )

    def bytes_of(ref, ssem, rsem):
        return remote(ref, ref, ssem, rsem, c=other)

    barrier = pltpu.get_barrier_semaphore()

    def greet(g=None, m=None, c=None):
        where = (grp if g is None else g, me if m is None else m, core if c is None else c)
        pl.semaphore_signal(barrier, inc=1, device_id=where, device_id_type=pl.DeviceIdType.MESH)

    for z in far_z:
        greet(m=z_at[z] + mx)
    for d in far_g:
        greet(g=g_at[d])
    for x in far_x:
        greet(m=z_at[0] + x_at[x])
    for m in (left, right):
        for c in (core, other):
            greet(m=m, c=c)
    greet(c=other)

    half_rows = OWNED // 2
    own_half = pl.ds(pl.multiple_of(core * half_rows, 8), half_rows)

    def table_rows(owner):
        return table.at[pl.ds(pl.multiple_of(owner * half_rows, 8), half_rows), :]

    def stage_rows(p, s, first, n):
        return stage.at[pl.ds(pl.multiple_of(p * (4 * STAGE) + s * STAGE + first, 8), n), :]

    own_table = pltpu.make_async_copy(ls_ref.at[own_half, :], table_rows(me), local_sem.at[1])
    own_table.start()
    own_src = [
        pltpu.make_async_copy(src_ref.at[4 * core + s], stage_rows(core, s, HALO, BLOCKS), local_sem.at[s + 2])
        for s in range(4)
    ]
    own_cells = [
        pltpu.make_async_copy(ref, self_v.at[k], local_sem.at[6 + k])
        for k, ref in enumerate((own_ref, slot_ref, rcv_ref))
    ]
    own_cpl = pltpu.make_async_copy(cpl_ref, cpl_v, local_sem.at[9])
    own_obs = pltpu.make_async_copy(obs_ref, obs_own.at[core], local_sem.at[0])
    for c in [own_cpl, own_obs] + own_cells + own_src:
        c.start()

    pl.semaphore_wait(barrier, nz - 1 + NX - 1 + ng - 1 + 5)

    for z in far_z:
        remote(ls_ref.at[own_half, :], table_rows(me), ag_send.at[0], ag_recv.at[mz], m=z_at[z] + mx).start()

    for side, m in ((0, right), (1, left)):
        for k, ref in enumerate((own_ref, slot_ref, rcv_ref)):
            remote(ref, near.at[side, k], small_send.at[0], small_recv.at[0], m=m).start()
    for s in range(4):
        remote(
            src_ref.at[4 * other + s], stage_rows(core, s, HALO, BLOCKS), ex_send.at[0], ex_recv.at[0], c=other
        ).start()
    obs_swap = remote(obs_ref, obs_own.at[core], ex_send.at[1], ex_recv.at[1], c=other)
    obs_swap.start()
    for side, m, first, into in ((0, right, BLOCKS - HALO, 0), (1, left, 0, STAGE - HALO)):
        for c in range(2):
            for s in range(4):
                remote(
                    src_ref.at[4 * c + s, pl.ds(first, HALO), :], stage_rows(core, s, into, HALO),
                    halo_send.at[0], halo_recv.at[0], m=m, c=c,
                ).start()
            remote(obs_ref, obs_near.at[side, core], obs_send.at[0], obs_recv.at[0], m=m, c=c).start()

    eye = iota((CELLS, CELLS), 0) == iota((CELLS, CELLS), 1)
    beside = jnp.abs(iota((CELLS, CELLS), 0) - iota((CELLS, CELLS), 1)) == 1
    own_cpl.wait()
    cpl = cpl_v[...]
    dinv = 1.0 / jnp.sum(jnp.where(eye, cpl, 0.0), axis=0, keepdims=True)
    for m, w in ((cpl.T, wf), (cpl, wa)):
        scaled = -dinv * (jnp.where(eye, 0.0, m) - jnp.where(beside, CHAIN, 0.0))
        hi, lo = two(scaled)
        w[0:CELLS, 0:CELLS] = hi
        w[0:CELLS, CELLS:] = lo
        w[CELLS:, 0:CELLS] = hi
        w[CELLS:, CELLS:] = lo

    for c in own_cells:
        c.wait()
    owner_row = self_v[0]
    slot_row = self_v[1]
    owner_col = column(owner_row.astype(f32)).astype(i32)
    earlier = (owner_col == owner_row) & (iota((BLOCKS, BLOCKS), 0) < iota((BLOCKS, BLOCKS), 1))
    rank = jnp.sum(jnp.where(earlier, 1.0, 0.0), axis=0, keepdims=True).astype(i32)
    place = owner_row * CAP + rank
    pick = jnp.where(iota((nm * CAP, BLOCKS), 0) == place, 1.0, 0.0)
    qmat[...] = pick.astype(bf16)
    slot_of = jnp.sum(pick * (slot_row + 1).astype(f32), axis=1, keepdims=True)
    slots[...] = jnp.broadcast_to(slot_of, (nm * CAP, CELLS)).reshape(nm, CAP, CELLS)

    own_table.wait()
    for z in [0] + far_z[::-1]:
        owner = z_at[z] + mx
        if z:
            remote(
                table_rows(owner), table_rows(owner), ag_send.at[0], ag_recv.at[lax.div(z_at[z], NX)], c=other
            ).wait_recv()
        for x in far_x:
            remote(
                table_rows(owner), table_rows(owner), fan_send.at[0], fan_recv.at[0], m=z_at[0] + x_at[x]
            ).start()

    bytes_of(near, small_send.at[0], small_recv.at[0]).wait_recv()
    own3 = jnp.concatenate([near[0, 0], owner_row, near[1, 0]] + [owner_row] * 5, axis=0)
    slot3 = jnp.concatenate([near[0, 1], slot_row, near[1, 1]] + [slot_row] * 5, axis=0)
    index_v[...] = own3 * half_rows + (slot3 & (half_rows - 1))
    to_scalars = pltpu.make_async_copy(index_v, index_s, index_sem)
    to_scalars.start()

    mine = jnp.where((slot3 >> 5) == core, 1.0, 0.0)
    wide = (HALO, BLOCKS)
    col_l = jnp.sum(jnp.where(iota(wide, 0) + BLOCKS - HALO == iota(wide, 1), mine[0:1], 0.0), axis=1, keepdims=True)
    col_r = jnp.sum(jnp.where(iota(wide, 0) == iota(wide, 1), mine[2:3], 0.0), axis=1, keepdims=True)
    choose[0:HALO, :] = jnp.broadcast_to(col_l, (HALO, CELLS))
    choose[HALO:HALO + BLOCKS, :] = jnp.broadcast_to(column(mine[1:2]), (BLOCKS, CELLS))
    choose[HALO + BLOCKS:, :] = jnp.broadcast_to(col_r, (HALO, CELLS))

    own_obs.wait()
    obs_swap.wait_recv()
    bytes_of(obs_near, obs_send.at[0], obs_recv.at[0]).wait_recv()
    odd = iota((8, CELLS), 0) % 2

    def receivers(cells, base, obs_at):
        block = (cells >> 7) + base - HALF * odd
        lane = jnp.where(iota((CELLS, CELLS), 0) == (cells & (CELLS - 1)), 1.0, 0.0).astype(bf16)
        values = []
        for p in range(2):
            rows = [obs_at[p, pl.ds(4 * core + s, 1), :] for s in range(4)]
            values.append(jnp.concatenate([rows[r // 2] for r in range(8)], axis=0))
        return block, lane, values

    def scatter(block, lane, values, i):
        at = jnp.tile(block, (8, 1)) == 8 * i + (iota((64, CELLS), 0) >> 3)
        twice = jnp.concatenate([lane, lane], axis=1)
        res = []
        for v in values:
            hi, lo = two(jnp.where(at, jnp.tile(v, (8, 1)), 0.0))
            res.append(dot_t(jnp.concatenate([hi, lo], axis=1), twice))
        return res, dot_t(jnp.where(at, 1.0, 0.0).astype(bf16), lane)

    here = receivers(self_v[2], HALO, obs_own)

    @pl.loop(0, HALF // 8)
    def _(i):
        res, cnt = scatter(*here, i)
        rows = pl.ds(pl.multiple_of(64 * i, 64), 64)
        heard[0, rows, :] = res[0]
        heard[1, rows, :] = res[1]
        count[rows, :] = cnt

    last = HALF // 8 - 1
    for side, base, i in ((0, HALO - BLOCKS, 0), (1, HALO + BLOCKS, last)):
        res, cnt = scatter(*receivers(near[side, 2], base, obs_near.at[side]), i)
        rows = slice(64 * i, 64 * i + 64)
        heard[0, rows, :] += res[0]
        heard[1, rows, :] += res[1]
        count[rows, :] += cnt

    for c in own_src:
        c.wait()
    bytes_of(stage.at[0:4 * BLOCKS, :], ex_send.at[0], ex_recv.at[0]).wait_recv()
    bytes_of(stage.at[0:16 * HALO, :], halo_send.at[0], halo_recv.at[0]).wait_recv()

    even_rows = iota((64, CELLS), 0) % 2 == 0
    keep_l = jnp.where(even_rows & (me == 0), 0.0, 1.0)
    keep_r = jnp.where(jnp.logical_not(even_rows) & (me == nm - 1), 0.0, 1.0)

    def kept(i, x):
        if isinstance(i, int):
            return x * keep_l if i == 0 else x * keep_r if i == last else x
        return x * jnp.where(i == 0, keep_l, jnp.where(i == last, keep_r, 1.0))

    def at64(i, first=0):
        return slice(first + 64 * i, first + 64 * i + 64) if isinstance(i, int) else pl.ds(
            pl.multiple_of(first + 64 * i, 8), 64)

    def put(b, p, i, x):
        b[p, at64(i, 8), :] = x
        hi, lo = two(x)
        lhs_hi[at64(2 * i + p), :] = hi
        lhs_lo[at64(2 * i + p), :] = lo

    def seams(b):
        top = iota((8, CELLS), 0) % 2 == 0
        for p in range(2):
            end = b[p, ROWS:ROWS + 8, :]
            start = b[p, 8:16, :]
            b[p, 0:8, :] = jnp.where(top, 0.0, pltpu.roll(end, 1, axis=0))
            b[p, ROWS + 8:ROWS + 16, :] = jnp.where(top, pltpu.roll(start, 7, axis=0), 0.0)

    @pl.loop(0, HALF // 8)
    def _(i):
        for p in range(2):
            x = jnp.concatenate(
                [stage[pl.ds(p * (4 * STAGE) + 8 * i + j, 8, stride=HALF), :] for j in range(8)], axis=0
            )
            x = kept(i, x * dinv)
            q[0, p, at64(i), :] = x
            put(fwd_a, p, i, x)

    seams(fwd_a)

    bytes_of(table.at[0:nz * (NX - 1) * half_rows, :], fan_send.at[0], fan_recv.at[0]).wait_recv()
    to_scalars.wait()

    def pick_rows(first, source, lane):
        picked[pl.ds(first, 8), :] = jnp.concatenate(
            [table[pl.ds(index_s[source, lane + j], 1), :] for j in range(8)], axis=0
        )

    pick_rows(0, 0, BLOCKS - HALO)
    pick_rows(HALO + BLOCKS, 2, 0)

    @pl.loop(0, BLOCKS // 8)
    def _(i):
        pick_rows(pl.multiple_of(HALO + 8 * i, 8), 1, 8 * i)

    swap = remote(picked, theirs, pick_send.at[0], pick_recv.at[0], c=other)
    swap.start()

    for z, x in far:
        m = z_at[z] + x_at[x]
        remote(slots.at[m], slots_in.at[me], sl_send.at[0], sl_recv.at[0], m=m).start()

    swap.wait_recv()
    wsig[...] = OMEGA * jnp.exp(jnp.where(choose[...] > 0.5, picked[...], theirs[...]))

    @pl.loop(0, HALF // 8)
    def _(i):
        rows = []
        for j in range(8):
            a = jnp.broadcast_to(wsig[pl.ds(8 * i + j, 1), :], (8, CELLS))
            b = jnp.broadcast_to(wsig[pl.ds(HALF + 8 * i + j, 1), :], (8, CELLS))
            rows.append(jnp.where(odd == 0, a, b))
        cross[at64(i), :] = kept(i, jnp.concatenate(rows, axis=0) * dinv)

    lane_row = iota((1, CELLS), 1)
    at_first = jnp.where(lane_row == 0, CHAIN * dinv, 0.0)
    at_last = jnp.where(lane_row == CELLS - 1, CHAIN * dinv, 0.0)

    def sweep(old, new, qk, sign, weights):
        for first in range(0, HALF // 8, GROUP):
            rows = slice(128 * first, 128 * (first + GROUP))
            prod = dot(jnp.concatenate([lhs_hi[rows, :], lhs_lo[rows, :]], axis=1), weights[...])
            prod = prod[:, 0:CELLS] + prod[:, CELLS:]
            for i in range(first, first + GROUP):
                turn = cross[at64(i), :]
                for p in range(2):
                    k = 2 * (i - first) + p
                    before = old[p, at64(i), :]
                    after = old[p, at64(i, 16), :]
                    both = turn * old[1 - p, at64(i, 8), :]
                    x = q[qk, p, at64(i), :] + prod[64 * k:64 * k + 64, :]
                    x = x + at_first * pltpu.roll(before, 1, axis=1) + at_last * pltpu.roll(after, CELLS - 1, axis=1)
                    x = x + both if (sign > 0) == (p == 0) else x - both
                    put(new, p, i, kept(i, x))
        seams(new)

    def sweeps(a, b, *args):
        sweep(a, b, *args)

        @pl.loop(0, ITERS // 2 - 1)
        def _(k):
            sweep(b, a, *args)
            sweep(a, b, *args)

    sweeps(fwd_a, fwd_b, 0, 1, wf)

    @pl.loop(0, HALF // 8)
    def _(i):
        for p in range(2):
            x = count[at64(i), :] * fwd_b[p, at64(i, 8), :] - heard[p, at64(i), :]
            x = kept(i, x * dinv)
            q[1, p, at64(i), :] = x
            put(adj_a, p, i, x)

    seams(adj_a)

    sweeps(adj_a, adj_b, 1, -1, wa)

    for i in range(HALF // 8):
        psum_buf[at64(i), :] = (
            adj_b[0, at64(i, 8), :] * fwd_b[1, at64(i, 8), :]
            - adj_b[1, at64(i, 8), :] * fwd_b[0, at64(i, 8), :]
        )

    for i in range(BLOCKS // 16):
        for h in range(2):
            first = 8 * (8 * i + (HALO if h == 0 else 0)) + h
            acc = psum_buf[pl.ds(first, 8, stride=8), :]
            for s in range(1, 4):
                acc = acc + psum_buf[pl.ds(first + 2 * s, 8, stride=8), :]
            at = 8 * i + (HALF - HALO) * h
            part[at:at + 8, :] = acc * wsig[HALO + at:HALO + at + 8, :]

    hi, mid, lo = three(part[...])
    sel = qmat[...]
    packed = dot(sel, hi) + dot(sel, mid) + dot(sel, lo)
    pack[...] = packed.reshape(nm, CAP, CELLS)

    for z, x in far:
        m = z_at[z] + x_at[x]
        remote(pack.at[m], pack_in.at[me], gp_send.at[0], gp_recv.at[0], m=m).start()

    pack_in[me] = pack[me]
    bytes_of(slots.at[0:nm - 1], sl_send.at[0], sl_recv.at[0]).wait_recv()
    slots_in[me] = slots[me]
    slot_in = slots_in[...].reshape(nm * CAP, CELLS)
    hit = jnp.where(slot_in == (iota((nm * CAP, CELLS), 1) + 1).astype(f32), 1.0, 0.0)
    hits[...] = hit.T.astype(bf16)

    bytes_of(table.at[0:(nz - 1) * half_rows, :], ag_send.at[0], ag_recv.at[0]).wait_send()
    bytes_of(near, small_send.at[0], small_recv.at[0]).wait_send()
    bytes_of(stage.at[0:4 * BLOCKS, :], ex_send.at[0], ex_recv.at[0]).wait_send()
    obs_swap.wait_send()
    bytes_of(stage.at[0:16 * HALO, :], halo_send.at[0], halo_recv.at[0]).wait_send()
    bytes_of(obs_near, obs_send.at[0], obs_recv.at[0]).wait_send()
    bytes_of(table.at[0:nz * (NX - 1) * half_rows, :], fan_send.at[0], fan_recv.at[0]).wait_send()
    swap.wait_send()
    bytes_of(slots.at[0:nm - 1], sl_send.at[0], sl_recv.at[0]).wait_send()

    bytes_of(pack.at[0:nm - 1], gp_send.at[0], gp_recv.at[0]).wait_recv()
    hi, mid, lo = three(pack_in[...].reshape(nm * CAP, CELLS))
    sel = hits[0:OWNED, :]
    grad[...] = dot(sel, hi) + dot(sel, mid) + dot(sel, lo)

    mine_half = pl.ds(pl.multiple_of(core * half_rows, 8), half_rows)
    their_half = pl.ds(pl.multiple_of(other * half_rows, 8), half_rows)
    cores = remote(grad.at[their_half, :], grad_in, gr_send.at[0], gr_recv.at[0], c=other)
    cores.start()
    cores.wait_recv()
    line[grp] = grad[mine_half, :] + grad_in[...]
    for d in far_g:
        remote(line.at[grp], line.at[grp], ln_send.at[0], ln_recv.at[0], g=g_at[d]).start()
    cores.wait_send()
    bytes_of(pack.at[0:nm - 1], gp_send.at[0], gp_recv.at[0]).wait_send()
    bytes_of(line.at[0:ng - 1], ln_send.at[0], ln_recv.at[0]).wait_recv()

    for k in range(2):
        summed = line[k * (ng // 2)]
        for g in range(k * (ng // 2) + 1, (k + 1) * (ng // 2)):
            summed = summed + line[g]
        total[k] = summed
    back = remote(total, total_in, to_send.at[0], to_recv.at[0], c=other)
    back.start()
    low_ref[mine_half, :] = total[0]
    high_ref[mine_half, :] = total[1]
    bytes_of(line.at[0:ng - 1], ln_send.at[0], ln_recv.at[0]).wait_send()
    back.wait()
    low_ref[their_half, :] = total_in[0]
    high_ref[their_half, :] = total_in[1]


def local(log_sigma, block_owner, block_slot, coupling, sources, rcv_cell, observed):
    nm, ng = lax.axis_size("mesh"), lax.axis_size("group")
    vmem, hbm, dma = pltpu.VMEM, pl.BlockSpec(memory_space=pl.ANY), pltpu.SemaphoreType.DMA
    inside = pl.BlockSpec(memory_space=pltpu.VMEM)
    nz = nm // NX
    low, high = pl.pallas_call(
        functools.partial(kernel, ng, nm),
        out_shape=[jax.ShapeDtypeStruct((OWNED, CELLS), f32)] * 2,
        in_specs=[hbm] * 7,
        out_specs=[inside] * 2,
        scratch_shapes=[
            vmem((8 * STAGE, CELLS), f32),
            vmem((nm * OWNED // 2, CELLS), f32),
            vmem((2, 3, 1, BLOCKS), i32),
            vmem((3, 1, BLOCKS), i32),
            vmem((CELLS, CELLS), f32),
            vmem((2, S, CELLS), f32),
            vmem((2, 2, S, CELLS), f32),
            vmem((8, BLOCKS), i32),
            pltpu.SMEM((8, BLOCKS), i32),
            vmem((STAGE, CELLS), f32),
            vmem((STAGE, CELLS), f32),
            vmem((STAGE, CELLS), f32),
            vmem((2, ROWS + 16, CELLS), f32),
            vmem((2, ROWS + 16, CELLS), f32),
            vmem((2, ROWS + 16, CELLS), f32),
            vmem((2, ROWS + 16, CELLS), f32),
            vmem((2 * ROWS, CELLS), bf16),
            vmem((2 * ROWS, CELLS), bf16),
            vmem((2, 2, ROWS, CELLS), f32),
            vmem((ROWS, CELLS), f32),
            vmem((STAGE, CELLS), f32),
            vmem((CELLS, nm * CAP), bf16),
            vmem((2, ROWS, CELLS), f32),
            vmem((ROWS, CELLS), f32),
            vmem((2 * CELLS, 2 * CELLS), bf16),
            vmem((2 * CELLS, 2 * CELLS), bf16),
            vmem((nm * CAP, BLOCKS), bf16),
            vmem((ROWS, CELLS), f32),
            vmem((BLOCKS, CELLS), f32),
            vmem((nm, CAP, CELLS), f32),
            vmem((nm, CAP, CELLS), f32),
            vmem((nm, CAP, CELLS), f32),
            vmem((nm, CAP, CELLS), f32),
            vmem((OWNED, CELLS), f32),
            vmem((OWNED // 2, CELLS), f32),
            vmem((ng, OWNED // 2, CELLS), f32),
            vmem((2, OWNED // 2, CELLS), f32),
            vmem((2, OWNED // 2, CELLS), f32),
            dma((10,)),
            dma((2,)), dma((2,)),
            dma((1,)), dma((1,)),
            dma((1,)), dma((1,)),
            dma((1,)), dma((1,)),
            dma((1,)), dma((nz,)),
            dma((1,)), dma((1,)),
            dma((1,)), dma((1,)),
            dma((1,)), dma((1,)),
            dma((1,)), dma((1,)),
            dma((1,)), dma((1,)),
            dma((1,)), dma((1,)),
            dma((1,)), dma((1,)),
            dma(()),
        ],
        compiler_params=pltpu.CompilerParams(collective_id=0, has_side_effects=True),
    )(
        block_owner.reshape(1, BLOCKS), block_slot, rcv_cell, observed.reshape(S, CELLS), coupling, log_sigma, sources.reshape(S, BLOCKS, CELLS)
    )
    return low + high


def solution(mesh):
    in_specs = (
        P("mesh", None),
        P("group", "mesh", None),
        P("group", "mesh"),
        P(),
        P("group", "comp", None, "mesh", None),
        P("group", "mesh"),
        P("group", "comp", None, "mesh"),
    )
    return jax.shard_map(local, mesh=mesh, in_specs=in_specs, out_specs=P("mesh", None), check_vma=False)
```

```python
import functools

import jax
import jax.numpy as jnp
from jax import lax
from jax.experimental import pallas as pl
from jax.experimental.pallas import tpu as pltpu
from jax.sharding import PartitionSpec as P

CELLS = 128
S = 8
ITERS = 6
CAP = 8
NX = 4
BLOCKS = 128
HALO = 8
HALF = (BLOCKS + 2 * HALO) // 2
ROWS = HALF * 8
STAGE = BLOCKS + 2 * HALO
OWNED = 64
GROUP = 9
OMEGA = 0.8
CHAIN = 1.0

f32, bf16, i32 = jnp.float32, jnp.bfloat16, jnp.int32
NT = (((1,), (1,)), ((), ()))


def iota(shape, dim):
    return lax.broadcasted_iota(i32, shape, dim)


def two(x):
    hi = x.astype(bf16)
    return hi, (x - hi.astype(f32)).astype(bf16)


def three(x):
    hi = x.astype(bf16)
    rest = x - hi.astype(f32)
    mid = rest.astype(bf16)
    return hi, mid, (rest - mid.astype(f32)).astype(bf16)


def dot(a, b):
    return jnp.dot(a, b, preferred_element_type=f32)


def dot_t(a, b):
    return lax.dot_general(a, b, NT, preferred_element_type=f32)


def cell_of(lane):
    return jnp.where(lane == CELLS // 2, CELLS - 1, jnp.where(lane == CELLS - 1, CELLS // 2, lane))


def reorder(x):
    lane = iota(x.shape, 1)
    up = pltpu.roll(x, CELLS // 2 + 1, axis=1)
    down = pltpu.roll(x, CELLS // 2 - 1, axis=1)
    return jnp.where(lane == CELLS // 2, up, jnp.where(lane == CELLS - 1, down, x))


def column(row):
    n = row.shape[1]
    return jnp.sum(jnp.where(iota((n, n), 0) == iota((n, n), 1), row, 0.0), axis=1, keepdims=True)


def kernel(
    ng, nm, own_ref, slot_ref, rcv_ref, obs_ref, cpl_ref, ls_ref, src_ref, out_ref,
    stage, table, near, self_v, cpl_v, obs_own, obs_near, index_v, index_s, picked, theirs, choose,
    fwd_a, fwd_b, adj_a, adj_b, lhs_hi, lhs_lo, q, cross, wsig, hits, heard, count, wf, wa, qmat, psum_buf, part,
    slots, slots_in, pack, pack_in, line, total, total_in,
    local_sem, ex_send, ex_recv, halo_send, halo_recv, obs_send, obs_recv, small_send, small_recv,
    ag_send, ag_recv, fan_send, fan_recv, pick_send, pick_recv, sl_send, sl_recv, gp_send, gp_recv,
    ln_send, ln_recv, to_send, to_recv, index_sem,
):
    me = lax.axis_index("mesh")
    core = lax.axis_index("comp")
    grp = lax.axis_index("group")
    other = 1 - core
    nz = nm // NX
    mz, mx = lax.div(me, NX), lax.rem(me, NX)
    z_at = [lax.rem(mz + d, nz) * NX for d in range(nz)]
    x_at = [lax.rem(mx + d, NX) for d in range(NX)]
    g_at = [lax.rem(grp + d, ng) for d in range(ng)]
    right, left = lax.rem(me + 1, nm), lax.rem(me + nm - 1, nm)

    def ring(d, n):
        return min(d, n - d)

    far_z, far_x, far_g = (sorted(range(1, n), key=lambda d: -ring(d, n)) for n in (nz, NX, ng))
    far = sorted(
        [(z, x) for z in range(nz) for x in range(NX) if z or x], key=lambda d: -ring(d[0], nz) - ring(d[1], NX)
    )

    def remote(src, dst, ssem, rsem, g=None, m=None, c=None):
        where = (grp if g is None else g, me if m is None else m, core if c is None else c)
        return pltpu.make_async_remote_copy(
            src_ref=src, dst_ref=dst, send_sem=ssem, recv_sem=rsem,
            device_id=where, device_id_type=pl.DeviceIdType.MESH,
        )

    def bytes_of(ref, ssem, rsem):
        return remote(ref, ref, ssem, rsem, c=other)

    barrier = pltpu.get_barrier_semaphore()

    def greet(g=None, m=None, c=None):
        where = (grp if g is None else g, me if m is None else m, core if c is None else c)
        pl.semaphore_signal(barrier, inc=1, device_id=where, device_id_type=pl.DeviceIdType.MESH)

    for z in far_z:
        greet(m=z_at[z] + mx)
    for d in far_g:
        greet(g=g_at[d])
    for x in far_x:
        greet(m=z_at[0] + x_at[x])
    for m in (left, right):
        for c in (core, other):
            greet(m=m, c=c)
    greet(c=other)

    half_rows = OWNED // 2
    own_half = pl.ds(pl.multiple_of(core * half_rows, 8), half_rows)

    def table_rows(owner):
        return table.at[pl.ds(pl.multiple_of(owner * half_rows, 8), half_rows), :]

    def stage_rows(p, s, first, n):
        return stage.at[pl.ds(pl.multiple_of(p * (4 * STAGE) + s * STAGE + first, 8), n), :]

    own_table = pltpu.make_async_copy(ls_ref.at[own_half, :], table_rows(me), local_sem.at[1])
    own_table.start()
    own_src = [
        pltpu.make_async_copy(src_ref.at[4 * core + s], stage_rows(core, s, HALO, BLOCKS), local_sem.at[s + 2])
        for s in range(4)
    ]
    own_cells = [
        pltpu.make_async_copy(ref, self_v.at[k], local_sem.at[6 + k])
        for k, ref in enumerate((own_ref, slot_ref, rcv_ref))
    ]
    own_cpl = pltpu.make_async_copy(cpl_ref, cpl_v, local_sem.at[9])
    own_obs = pltpu.make_async_copy(obs_ref, obs_own.at[core], local_sem.at[0])
    for c in [own_cpl, own_obs] + own_cells + own_src:
        c.start()

    pl.semaphore_wait(barrier, nz - 1 + NX - 1 + ng - 1 + 5)

    for z in far_z[::-1]:
        remote(ls_ref.at[own_half, :], table_rows(me), ag_send.at[0], ag_recv.at[mz], m=z_at[z] + mx).start()

    for side, m in ((0, right), (1, left)):
        for k, ref in enumerate((own_ref, slot_ref, rcv_ref)):
            remote(ref, near.at[side, k], small_send.at[0], small_recv.at[0], m=m).start()
    for s in range(4):
        remote(
            src_ref.at[4 * other + s], stage_rows(core, s, HALO, BLOCKS), ex_send.at[0], ex_recv.at[0], c=other
        ).start()
    obs_swap = remote(obs_ref, obs_own.at[core], ex_send.at[1], ex_recv.at[1], c=other)
    obs_swap.start()
    for side, m, first, into in ((0, right, BLOCKS - HALO, 0), (1, left, 0, STAGE - HALO)):
        for c in range(2):
            for s in range(4):
                remote(
                    src_ref.at[4 * c + s, pl.ds(first, HALO), :], stage_rows(core, s, into, HALO),
                    halo_send.at[0], halo_recv.at[0], m=m, c=c,
                ).start()
            remote(obs_ref, obs_near.at[side, core], obs_send.at[0], obs_recv.at[0], m=m, c=c).start()

    eye = iota((CELLS, CELLS), 0) == iota((CELLS, CELLS), 1)
    square = (CELLS, CELLS)
    beside = jnp.abs(cell_of(iota(square, 0)) - cell_of(iota(square, 1))) == 1
    own_cpl.wait()
    cpl_v[...] = reorder(cpl_v[...])
    mid_row, last_row = cpl_v[CELLS // 2:CELLS // 2 + 1, :], cpl_v[CELLS - 1:, :]
    cpl_v[CELLS // 2:CELLS // 2 + 1, :] = last_row
    cpl_v[CELLS - 1:, :] = mid_row
    cpl = cpl_v[...]
    dinv = 1.0 / jnp.sum(jnp.where(eye, cpl, 0.0), axis=0, keepdims=True)
    for m, w in ((cpl.T, wf), (cpl, wa)):
        scaled = -dinv * (jnp.where(eye, 0.0, m) - jnp.where(beside, CHAIN, 0.0))
        hi, lo = two(scaled)
        w[0:CELLS, 0:CELLS] = hi
        w[0:CELLS, CELLS:] = lo
        w[CELLS:, 0:CELLS] = hi
        w[CELLS:, CELLS:] = lo

    for c in own_cells:
        c.wait()
    owner_row = self_v[0]
    slot_row = self_v[1]
    owner_col = column(owner_row.astype(f32)).astype(i32)
    earlier = (owner_col == owner_row) & (iota((BLOCKS, BLOCKS), 0) < iota((BLOCKS, BLOCKS), 1))
    rank = jnp.sum(jnp.where(earlier, 1.0, 0.0), axis=0, keepdims=True).astype(i32)
    place = owner_row * CAP + rank
    pick = jnp.where(iota((nm * CAP, BLOCKS), 0) == place, 1.0, 0.0)
    qmat[...] = pick.astype(bf16)
    slot_of = jnp.sum(pick * (slot_row + 1).astype(f32), axis=1, keepdims=True)
    slots[...] = jnp.broadcast_to(slot_of, (nm * CAP, CELLS)).reshape(nm, CAP, CELLS)

    own_table.wait()
    for z in [0] + far_z[::-1]:
        owner = z_at[z] + mx
        if z:
            remote(
                table_rows(owner), table_rows(owner), ag_send.at[0], ag_recv.at[lax.div(z_at[z], NX)], c=other
            ).wait_recv()
        for x in far_x:
            remote(
                table_rows(owner), table_rows(owner), fan_send.at[0], fan_recv.at[0], m=z_at[0] + x_at[x]
            ).start()

    bytes_of(near, small_send.at[0], small_recv.at[0]).wait_recv()
    own3 = jnp.concatenate([near[0, 0], owner_row, near[1, 0]] + [owner_row] * 5, axis=0)
    slot3 = jnp.concatenate([near[0, 1], slot_row, near[1, 1]] + [slot_row] * 5, axis=0)
    index_v[...] = own3 * half_rows + (slot3 & (half_rows - 1))
    to_scalars = pltpu.make_async_copy(index_v, index_s, index_sem)
    to_scalars.start()

    mine = jnp.where((slot3 >> 5) == core, 1.0, 0.0)
    wide = (HALO, BLOCKS)
    col_l = jnp.sum(jnp.where(iota(wide, 0) + BLOCKS - HALO == iota(wide, 1), mine[0:1], 0.0), axis=1, keepdims=True)
    col_r = jnp.sum(jnp.where(iota(wide, 0) == iota(wide, 1), mine[2:3], 0.0), axis=1, keepdims=True)
    choose[0:HALO, :] = jnp.broadcast_to(col_l, (HALO, CELLS))
    choose[HALO:HALO + BLOCKS, :] = jnp.broadcast_to(column(mine[1:2]), (BLOCKS, CELLS))
    choose[HALO + BLOCKS:, :] = jnp.broadcast_to(col_r, (HALO, CELLS))

    own_obs.wait()
    obs_swap.wait_recv()
    bytes_of(obs_near, obs_send.at[0], obs_recv.at[0]).wait_recv()
    odd = iota((8, CELLS), 0) % 2

    def receivers(cells, base, obs_at):
        block = (cells >> 7) + base - HALF * odd
        lane = jnp.where(cell_of(iota(square, 0)) == (cells & (CELLS - 1)), 1.0, 0.0).astype(bf16)
        values = []
        for p in range(2):
            rows = [obs_at[p, pl.ds(4 * core + s, 1), :] for s in range(4)]
            values.append(jnp.concatenate([rows[r // 2] for r in range(8)], axis=0))
        return block, lane, values

    def scatter(block, lane, values, i):
        at = jnp.tile(block, (8, 1)) == 8 * i + (iota((64, CELLS), 0) >> 3)
        twice = jnp.concatenate([lane, lane], axis=1)
        res = []
        for v in values:
            hi, lo = two(jnp.where(at, jnp.tile(v, (8, 1)), 0.0))
            res.append(dot_t(jnp.concatenate([hi, lo], axis=1), twice))
        return res, dot_t(jnp.where(at, 1.0, 0.0).astype(bf16), lane)

    here = receivers(self_v[2], HALO, obs_own)

    @pl.loop(0, HALF // 8)
    def _(i):
        res, cnt = scatter(*here, i)
        rows = pl.ds(pl.multiple_of(64 * i, 64), 64)
        heard[0, rows, :] = res[0]
        heard[1, rows, :] = res[1]
        count[rows, :] = cnt

    last = HALF // 8 - 1
    for side, base, i in ((0, HALO - BLOCKS, 0), (1, HALO + BLOCKS, last)):
        res, cnt = scatter(*receivers(near[side, 2], base, obs_near.at[side]), i)
        rows = slice(64 * i, 64 * i + 64)
        heard[0, rows, :] += res[0]
        heard[1, rows, :] += res[1]
        count[rows, :] += cnt

    for c in own_src:
        c.wait()
    bytes_of(stage.at[0:4 * BLOCKS, :], ex_send.at[0], ex_recv.at[0]).wait_recv()
    bytes_of(stage.at[0:16 * HALO, :], halo_send.at[0], halo_recv.at[0]).wait_recv()

    even_rows = iota((64, CELLS), 0) % 2 == 0
    keep_l = jnp.where(even_rows & (me == 0), 0.0, 1.0)
    keep_r = jnp.where(jnp.logical_not(even_rows) & (me == nm - 1), 0.0, 1.0)

    def kept(i, x):
        if isinstance(i, int):
            return x * keep_l if i == 0 else x * keep_r if i == last else x
        return x * jnp.where(i == 0, keep_l, jnp.where(i == last, keep_r, 1.0))

    def at64(i, first=0):
        return slice(first + 64 * i, first + 64 * i + 64) if isinstance(i, int) else pl.ds(
            pl.multiple_of(first + 64 * i, 8), 64)

    def put(b, p, i, x):
        b[p, at64(i, 8), :] = x
        hi, lo = two(x)
        lhs_hi[at64(2 * i + p), :] = hi
        lhs_lo[at64(2 * i + p), :] = lo

    def seams(b):
        top = iota((8, CELLS), 0) % 2 == 0
        for p in range(2):
            end = b[p, ROWS:ROWS + 8, :]
            start = b[p, 8:16, :]
            b[p, 0:8, :] = jnp.where(top, 0.0, pltpu.roll(end, 1, axis=0))
            b[p, ROWS + 8:ROWS + 16, :] = jnp.where(top, pltpu.roll(start, 7, axis=0), 0.0)

    @pl.loop(0, HALF // 8)
    def _(i):
        for p in range(2):
            x = jnp.concatenate(
                [stage[pl.ds(p * (4 * STAGE) + 8 * i + j, 8, stride=HALF), :] for j in range(8)], axis=0
            )
            x = kept(i, reorder(x) * dinv)
            q[0, p, at64(i), :] = x
            put(fwd_a, p, i, x)

    seams(fwd_a)

    bytes_of(table.at[0:nz * (NX - 1) * half_rows, :], fan_send.at[0], fan_recv.at[0]).wait_recv()
    to_scalars.wait()

    def pick_rows(first, source, lane):
        picked[pl.ds(first, 8), :] = jnp.concatenate(
            [table[pl.ds(index_s[source, lane + j], 1), :] for j in range(8)], axis=0
        )

    pick_rows(0, 0, BLOCKS - HALO)
    pick_rows(HALO + BLOCKS, 2, 0)

    for i in range(BLOCKS // 8):
        pick_rows(HALO + 8 * i, 1, 8 * i)

    swap = remote(picked, theirs, pick_send.at[0], pick_recv.at[0], c=other)
    swap.start()

    for z, x in far:
        m = z_at[z] + x_at[x]
        remote(slots.at[m], slots_in.at[me], sl_send.at[0], sl_recv.at[0], m=m).start()

    swap.wait_recv()
    wsig[...] = OMEGA * jnp.exp(reorder(jnp.where(choose[...] > 0.5, picked[...], theirs[...])))

    for i in range(HALF // 8):
        rows = []
        for j in range(8):
            a = jnp.broadcast_to(wsig[pl.ds(8 * i + j, 1), :], (8, CELLS))
            b = jnp.broadcast_to(wsig[pl.ds(HALF + 8 * i + j, 1), :], (8, CELLS))
            rows.append(jnp.where(odd == 0, a, b))
        cross[at64(i), :] = kept(i, jnp.concatenate(rows, axis=0) * dinv)

    lane_row = iota((1, CELLS), 1)
    ends = jnp.where((lane_row == 0) | (lane_row == CELLS // 2), CHAIN * dinv, 0.0)
    low_lane = iota((64, CELLS), 1) < CELLS // 4

    def sweep(old, new, qk, sign, weights):
        for first in range(0, HALF // 8, GROUP):
            rows = slice(128 * first, 128 * (first + GROUP))
            prod = dot(jnp.concatenate([lhs_hi[rows, :], lhs_lo[rows, :]], axis=1), weights[...])
            prod = prod[:, 0:CELLS] + prod[:, CELLS:]
            for i in range(first, first + GROUP):
                turn = cross[at64(i), :]
                near_x = [old[p, 64 * i:64 * i + 80, :] for p in range(2)]
                for p in range(2):
                    k = 2 * (i - first) + p
                    end = jnp.where(low_lane, near_x[p][16:80], near_x[p][0:64])
                    both = turn * near_x[1 - p][8:72]
                    x = q[qk, p, at64(i), :] + prod[64 * k:64 * k + 64, :] + ends * pltpu.roll(end, CELLS // 2, axis=1)
                    x = x + both if (sign > 0) == (p == 0) else x - both
                    put(new, p, i, kept(i, x))
        seams(new)

    def sweeps(a, b, *args):
        sweep(a, b, *args)

        @pl.loop(0, ITERS // 2 - 1)
        def _(k):
            sweep(b, a, *args)
            sweep(a, b, *args)

    sweeps(fwd_a, fwd_b, 0, 1, wf)

    for i in range(HALF // 8):
        for p in range(2):
            x = count[at64(i), :] * fwd_b[p, at64(i, 8), :] - heard[p, at64(i), :]
            x = kept(i, x * dinv)
            q[1, p, at64(i), :] = x
            put(adj_a, p, i, x)

    seams(adj_a)

    sweeps(adj_a, adj_b, 1, -1, wa)

    for i in range(HALF // 8):
        psum_buf[at64(i), :] = (
            adj_b[0, at64(i, 8), :] * fwd_b[1, at64(i, 8), :]
            - adj_b[1, at64(i, 8), :] * fwd_b[0, at64(i, 8), :]
        )

    for i in range(BLOCKS // 16):
        for h in range(2):
            first = 8 * (8 * i + (HALO if h == 0 else 0)) + h
            acc = psum_buf[pl.ds(first, 8, stride=8), :]
            for s in range(1, 4):
                acc = acc + psum_buf[pl.ds(first + 2 * s, 8, stride=8), :]
            at = 8 * i + (HALF - HALO) * h
            part[at:at + 8, :] = acc * wsig[HALO + at:HALO + at + 8, :]

    hi, mid, lo = three(reorder(part[...]))
    sel = qmat[...]
    packed = dot(sel, hi) + dot(sel, mid) + dot(sel, lo)
    pack[...] = packed.reshape(nm, CAP, CELLS)

    takes = lax.rem(mx, 2) == core
    for z, x in far:
        m = z_at[z] + x_at[x]
        remote(
            pack.at[m], pack_in.at[core * nm + me], gp_send.at[0], gp_recv.at[0], m=m, c=lax.rem(x_at[x], 2)
        ).start()
    beside_me = remote(pack.at[me], pack_in.at[core * nm + me], gp_send.at[1], gp_recv.at[0], c=other)

    @pl.when(jnp.logical_not(takes))
    def _():
        beside_me.start()

    @pl.when(takes)
    def _():
        pack_in[core * nm + me] = pack[me]

    bytes_of(slots.at[0:nm - 1], sl_send.at[0], sl_recv.at[0]).wait_recv()
    slots_in[me] = slots[me]

    bytes_of(table.at[0:(nz - 1) * half_rows, :], ag_send.at[0], ag_recv.at[0]).wait_send()
    bytes_of(near, small_send.at[0], small_recv.at[0]).wait_send()
    bytes_of(stage.at[0:4 * BLOCKS, :], ex_send.at[0], ex_recv.at[0]).wait_send()
    obs_swap.wait_send()
    bytes_of(stage.at[0:16 * HALO, :], halo_send.at[0], halo_recv.at[0]).wait_send()
    bytes_of(obs_near, obs_send.at[0], obs_recv.at[0]).wait_send()
    bytes_of(table.at[0:nz * (NX - 1) * half_rows, :], fan_send.at[0], fan_recv.at[0]).wait_send()
    swap.wait_send()
    bytes_of(slots.at[0:nm - 1], sl_send.at[0], sl_recv.at[0]).wait_send()

    back = remote(total, total_in, to_send.at[0], to_recv.at[0], c=other)

    @pl.when(takes)
    def _():
        slot_in = slots_in[...].reshape(nm * CAP, CELLS)
        hit = jnp.where(slot_in == (iota((nm * CAP, CELLS), 1) + 1).astype(f32), 1.0, 0.0)
        hits[...] = hit.T.astype(bf16)

        bytes_of(pack_in.at[0:2 * nm - 1], gp_send.at[0], gp_recv.at[0]).wait_recv()
        rows = (pack_in[0:nm] + pack_in[nm:2 * nm]).reshape(nm * CAP, CELLS)
        hi, mid, lo = three(rows)
        sel = hits[0:OWNED, :]
        line[grp] = dot(sel, hi) + dot(sel, mid) + dot(sel, lo)

        for d in far_g:
            remote(line.at[grp], line.at[grp], ln_send.at[0], ln_recv.at[0], g=g_at[d]).start()
        bytes_of(line.at[0:ng - 1], ln_send.at[0], ln_recv.at[0]).wait_recv()
        summed = line[0]
        for g in range(1, ng):
            summed = summed + line[g]
        total[...] = summed
        back.start()
        out_ref[...] = summed
        bytes_of(line.at[0:ng - 1], ln_send.at[0], ln_recv.at[0]).wait_send()
        back.wait_send()

    @pl.when(jnp.logical_not(takes))
    def _():
        beside_me.wait_send()
        back.wait_recv()
        out_ref[...] = total_in[...]

    bytes_of(pack.at[0:nm - 1], gp_send.at[0], gp_recv.at[0]).wait_send()


def local(log_sigma, block_owner, block_slot, coupling, sources, rcv_cell, observed):
    nm, ng = lax.axis_size("mesh"), lax.axis_size("group")
    vmem, hbm, dma = pltpu.VMEM, pl.BlockSpec(memory_space=pl.ANY), pltpu.SemaphoreType.DMA
    inside = pl.BlockSpec(memory_space=pltpu.VMEM)
    nz = nm // NX
    return pl.pallas_call(
        functools.partial(kernel, ng, nm),
        out_shape=pltpu.VMEM((OWNED, CELLS), f32),
        in_specs=[hbm] * 7,
        out_specs=inside,
        scratch_shapes=[
            vmem((8 * STAGE, CELLS), f32),
            vmem((nm * OWNED // 2, CELLS), f32),
            vmem((2, 3, 1, BLOCKS), i32),
            vmem((3, 1, BLOCKS), i32),
            vmem((CELLS, CELLS), f32),
            vmem((2, S, CELLS), f32),
            vmem((2, 2, S, CELLS), f32),
            vmem((8, BLOCKS), i32),
            pltpu.SMEM((8, BLOCKS), i32),
            vmem((STAGE, CELLS), f32),
            vmem((STAGE, CELLS), f32),
            vmem((STAGE, CELLS), f32),
            vmem((2, ROWS + 16, CELLS), f32),
            vmem((2, ROWS + 16, CELLS), f32),
            vmem((2, ROWS + 16, CELLS), f32),
            vmem((2, ROWS + 16, CELLS), f32),
            vmem((2 * ROWS, CELLS), bf16),
            vmem((2 * ROWS, CELLS), bf16),
            vmem((2, 2, ROWS, CELLS), f32),
            vmem((ROWS, CELLS), f32),
            vmem((STAGE, CELLS), f32),
            vmem((CELLS, nm * CAP), bf16),
            vmem((2, ROWS, CELLS), f32),
            vmem((ROWS, CELLS), f32),
            vmem((2 * CELLS, 2 * CELLS), bf16),
            vmem((2 * CELLS, 2 * CELLS), bf16),
            vmem((nm * CAP, BLOCKS), bf16),
            vmem((ROWS, CELLS), f32),
            vmem((BLOCKS, CELLS), f32),
            vmem((nm, CAP, CELLS), f32),
            vmem((nm, CAP, CELLS), f32),
            vmem((nm, CAP, CELLS), f32),
            vmem((2 * nm, CAP, CELLS), f32),
            vmem((ng, OWNED, CELLS), f32),
            vmem((OWNED, CELLS), f32),
            vmem((OWNED, CELLS), f32),
            dma((10,)),
            dma((2,)), dma((2,)),
            dma((1,)), dma((1,)),
            dma((1,)), dma((1,)),
            dma((1,)), dma((1,)),
            dma((1,)), dma((nz,)),
            dma((1,)), dma((1,)),
            dma((1,)), dma((1,)),
            dma((1,)), dma((1,)),
            dma((2,)), dma((1,)),
            dma((1,)), dma((1,)),
            dma((1,)), dma((1,)),
            dma(()),
        ],
        compiler_params=pltpu.CompilerParams(collective_id=0, has_side_effects=True),
    )(
        block_owner.reshape(1, BLOCKS), block_slot, rcv_cell, observed.reshape(S, CELLS), coupling, log_sigma, sources.reshape(S, BLOCKS, CELLS)
    )


def solution(mesh):
    in_specs = (
        P("mesh", None),
        P("group", "mesh", None),
        P("group", "mesh"),
        P(),
        P("group", "comp", None, "mesh", None),
        P("group", "mesh"),
        P("group", "comp", None, "mesh"),
    )
    return jax.shard_map(local, mesh=mesh, in_specs=in_specs, out_specs=P("mesh", None), check_vma=False)
```

```python
import functools

import jax
import jax.numpy as jnp
from jax import lax
from jax.experimental import pallas as pl
from jax.experimental.pallas import tpu as pltpu
from jax.sharding import PartitionSpec as P

CELLS = 128
S = 8
ITERS = 6
CAP = 8
NX = 4
BLOCKS = 128
HALO = 8
HALF = (BLOCKS + 2 * HALO) // 2
ROWS = HALF * 8
STAGE = BLOCKS + 2 * HALO
OWNED = 64
GROUPS = ((0, 3), (3, 6), (6, 9))
OMEGA = 0.8
CHAIN = 1.0

f32, bf16, i32 = jnp.float32, jnp.bfloat16, jnp.int32
NT = (((1,), (1,)), ((), ()))


def iota(shape, dim):
    return lax.broadcasted_iota(i32, shape, dim)


def two(x):
    hi = x.astype(bf16)
    return hi, (x - hi.astype(f32)).astype(bf16)


def three(x):
    hi = x.astype(bf16)
    rest = x - hi.astype(f32)
    mid = rest.astype(bf16)
    return hi, mid, (rest - mid.astype(f32)).astype(bf16)


def dot(a, b):
    return jnp.dot(a, b, preferred_element_type=f32)


def dot_t(a, b):
    return lax.dot_general(a, b, NT, preferred_element_type=f32)


def cell_of(lane):
    return jnp.where(lane == CELLS // 2, CELLS - 1, jnp.where(lane == CELLS - 1, CELLS // 2, lane))


def reorder(x):
    lane = iota(x.shape, 1)
    up = pltpu.roll(x, CELLS // 2 + 1, axis=1)
    down = pltpu.roll(x, CELLS // 2 - 1, axis=1)
    return jnp.where(lane == CELLS // 2, up, jnp.where(lane == CELLS - 1, down, x))


def column(row):
    n = row.shape[1]
    return jnp.sum(jnp.where(iota((n, n), 0) == iota((n, n), 1), row, 0.0), axis=1, keepdims=True)


def kernel(
    ng, nm, own_ref, slot_ref, rcv_ref, obs_ref, cpl_ref, ls_ref, src_ref, out_ref,
    stage, table, near, self_v, cpl_v, obs_own, obs_near, index_v, index_s, picked, theirs, choose,
    fwd_a, fwd_b, adj_a, adj_b, lhs_hi, lhs_lo, q, cross, wsig, hits, heard, count, wf, wa, qmat, psum_buf, part,
    slots, slots_in, pack, pack_in, line, total, total_in,
    local_sem, ex_send, ex_recv, halo_send, halo_recv, obs_send, obs_recv, small_send, small_recv,
    ag_send, ag_recv, fan_send, fan_recv, pick_send, pick_recv, sl_send, sl_recv, gp_send, gp_recv,
    ln_send, ln_recv, to_send, to_recv, index_sem,
):
    me = lax.axis_index("mesh")
    core = lax.axis_index("comp")
    grp = lax.axis_index("group")
    other = 1 - core
    nz = nm // NX
    mz, mx = lax.div(me, NX), lax.rem(me, NX)
    z_at = [lax.rem(mz + d, nz) * NX for d in range(nz)]
    x_at = [lax.rem(mx + d, NX) for d in range(NX)]
    g_at = [lax.rem(grp + d, ng) for d in range(ng)]
    right, left = lax.rem(me + 1, nm), lax.rem(me + nm - 1, nm)

    def ring(d, n):
        return min(d, n - d)

    far_z, far_x, far_g = (sorted(range(1, n), key=lambda d: -ring(d, n)) for n in (nz, NX, ng))
    far = sorted(
        [(z, x) for z in range(nz) for x in range(NX) if z or x], key=lambda d: -ring(d[0], nz) - ring(d[1], NX)
    )

    def remote(src, dst, ssem, rsem, g=None, m=None, c=None):
        where = (grp if g is None else g, me if m is None else m, core if c is None else c)
        return pltpu.make_async_remote_copy(
            src_ref=src, dst_ref=dst, send_sem=ssem, recv_sem=rsem,
            device_id=where, device_id_type=pl.DeviceIdType.MESH,
        )

    def bytes_of(ref, ssem, rsem):
        return remote(ref, ref, ssem, rsem, c=other)

    barrier = pltpu.get_barrier_semaphore()

    def greet(g=None, m=None, c=None):
        where = (grp if g is None else g, me if m is None else m, core if c is None else c)
        pl.semaphore_signal(barrier, inc=1, device_id=where, device_id_type=pl.DeviceIdType.MESH)

    for z in far_z:
        greet(m=z_at[z] + mx)
    for d in far_g:
        greet(g=g_at[d])
    for x in far_x:
        greet(m=z_at[0] + x_at[x])
    for m in (left, right):
        for c in (core, other):
            greet(m=m, c=c)
    greet(c=other)

    half_rows = OWNED // 2
    own_half = pl.ds(pl.multiple_of(core * half_rows, 8), half_rows)

    def table_rows(owner):
        return table.at[pl.ds(pl.multiple_of(owner * half_rows, 8), half_rows), :]

    def stage_rows(p, s, first, n):
        return stage.at[pl.ds(pl.multiple_of(p * (4 * STAGE) + s * STAGE + first, 8), n), :]

    own_table = pltpu.make_async_copy(ls_ref.at[own_half, :], table_rows(me), local_sem.at[1])
    own_table.start()
    own_src = [
        pltpu.make_async_copy(src_ref.at[4 * core + s], stage_rows(core, s, HALO, BLOCKS), local_sem.at[s + 2])
        for s in range(4)
    ]
    own_cells = [
        pltpu.make_async_copy(ref, self_v.at[k], local_sem.at[6 + k])
        for k, ref in enumerate((own_ref, slot_ref, rcv_ref))
    ]
    own_cpl = pltpu.make_async_copy(cpl_ref, cpl_v, local_sem.at[9])
    own_obs = pltpu.make_async_copy(obs_ref, obs_own.at[core], local_sem.at[0])
    for c in [own_cpl, own_obs] + own_cells + own_src:
        c.start()

    pl.semaphore_wait(barrier, nz - 1 + NX - 1 + ng - 1 + 5)

    for z in far_z[::-1]:
        remote(ls_ref.at[own_half, :], table_rows(me), ag_send.at[0], ag_recv.at[mz], m=z_at[z] + mx).start()

    for x in far_x:
        remote(
            ls_ref.at[own_half, :], table_rows(me), fan_send.at[0], fan_recv.at[0], m=z_at[0] + x_at[x]
        ).start()

    for side, m in ((0, right), (1, left)):
        for k, ref in enumerate((own_ref, slot_ref, rcv_ref)):
            remote(ref, near.at[side, k], small_send.at[0], small_recv.at[0], m=m).start()
    for s in range(4):
        remote(
            src_ref.at[4 * other + s], stage_rows(core, s, HALO, BLOCKS), ex_send.at[0], ex_recv.at[0], c=other
        ).start()
    obs_swap = remote(obs_ref, obs_own.at[core], ex_send.at[1], ex_recv.at[1], c=other)
    obs_swap.start()
    for side, m, first, into in ((0, right, BLOCKS - HALO, 0), (1, left, 0, STAGE - HALO)):
        for c in range(2):
            for s in range(4):
                remote(
                    src_ref.at[4 * c + s, pl.ds(first, HALO), :], stage_rows(core, s, into, HALO),
                    halo_send.at[0], halo_recv.at[0], m=m, c=c,
                ).start()
            remote(obs_ref, obs_near.at[side, core], obs_send.at[0], obs_recv.at[0], m=m, c=c).start()

    eye = iota((CELLS, CELLS), 0) == iota((CELLS, CELLS), 1)
    square = (CELLS, CELLS)
    beside = jnp.abs(cell_of(iota(square, 0)) - cell_of(iota(square, 1))) == 1
    own_cpl.wait()
    cpl_v[...] = reorder(cpl_v[...])
    mid_row, last_row = cpl_v[CELLS // 2:CELLS // 2 + 1, :], cpl_v[CELLS - 1:, :]
    cpl_v[CELLS // 2:CELLS // 2 + 1, :] = last_row
    cpl_v[CELLS - 1:, :] = mid_row
    cpl = cpl_v[...]
    dinv = 1.0 / jnp.sum(jnp.where(eye, cpl, 0.0), axis=0, keepdims=True)
    for m, w in ((cpl.T, wf), (cpl, wa)):
        scaled = -dinv * (jnp.where(eye, 0.0, m) - jnp.where(beside, CHAIN, 0.0))
        hi, lo = two(scaled)
        w[0:CELLS, 0:CELLS] = hi
        w[0:CELLS, CELLS:] = lo
        w[CELLS:, 0:CELLS] = hi
        w[CELLS:, CELLS:] = lo

    for c in own_cells:
        c.wait()
    owner_row = self_v[0]
    slot_row = self_v[1]
    owner_col = column(owner_row.astype(f32)).astype(i32)
    earlier = (owner_col == owner_row) & (iota((BLOCKS, BLOCKS), 0) < iota((BLOCKS, BLOCKS), 1))
    rank = jnp.sum(jnp.where(earlier, 1.0, 0.0), axis=0, keepdims=True).astype(i32)
    place = owner_row * CAP + rank
    pick = jnp.where(iota((nm * CAP, BLOCKS), 0) == place, 1.0, 0.0)
    qmat[...] = pick.astype(bf16)
    slot_of = jnp.sum(pick * (slot_row + 1).astype(f32), axis=1, keepdims=True)
    slots[...] = jnp.broadcast_to(slot_of, (nm * CAP, CELLS)).reshape(nm, CAP, CELLS)

    def relay(owner, k, m):
        remote(table_rows(owner), table_rows(owner), fan_send.at[0], fan_recv.at[k], m=m).start()

    def along_z(z):
        owner = z_at[z] + mx
        remote(
            table_rows(owner), table_rows(owner), ag_send.at[0], ag_recv.at[lax.div(z_at[z], NX)], c=other
        ).wait_recv()
        return owner

    near_z = far_z[1:][::-1]
    for z in near_z[:2]:
        owner = along_z(z)
        for x in far_x:
            relay(owner, 1, z_at[0] + x_at[x])
    bytes_of(table.at[0:(NX - 1) * half_rows, :], fan_send.at[0], fan_recv.at[0]).wait_recv()
    for x in far_x[::-1]:
        relay(z_at[0] + x_at[x], 1, z_at[far_z[0]] + mx)
    for z in near_z[2:]:
        owner = along_z(z)
        for x in far_x:
            relay(owner, 1, z_at[0] + x_at[x])
    along_z(far_z[0])

    bytes_of(near, small_send.at[0], small_recv.at[0]).wait_recv()
    own3 = jnp.concatenate([near[0, 0], owner_row, near[1, 0]] + [owner_row] * 5, axis=0)
    slot3 = jnp.concatenate([near[0, 1], slot_row, near[1, 1]] + [slot_row] * 5, axis=0)
    index_v[...] = own3 * half_rows + (slot3 & (half_rows - 1))
    to_scalars = pltpu.make_async_copy(index_v, index_s, index_sem)
    to_scalars.start()

    mine = jnp.where((slot3 >> 5) == core, 1.0, 0.0)
    wide = (HALO, BLOCKS)
    col_l = jnp.sum(jnp.where(iota(wide, 0) + BLOCKS - HALO == iota(wide, 1), mine[0:1], 0.0), axis=1, keepdims=True)
    col_r = jnp.sum(jnp.where(iota(wide, 0) == iota(wide, 1), mine[2:3], 0.0), axis=1, keepdims=True)
    choose[0:HALO, :] = jnp.broadcast_to(col_l, (HALO, CELLS))
    choose[HALO:HALO + BLOCKS, :] = jnp.broadcast_to(column(mine[1:2]), (BLOCKS, CELLS))
    choose[HALO + BLOCKS:, :] = jnp.broadcast_to(col_r, (HALO, CELLS))

    own_obs.wait()
    obs_swap.wait_recv()
    bytes_of(obs_near, obs_send.at[0], obs_recv.at[0]).wait_recv()
    odd = iota((8, CELLS), 0) % 2

    def receivers(cells, base, obs_at):
        block = (cells >> 7) + base - HALF * odd
        lane = jnp.where(cell_of(iota(square, 0)) == (cells & (CELLS - 1)), 1.0, 0.0).astype(bf16)
        values = []
        for p in range(2):
            rows = [obs_at[p, pl.ds(4 * core + s, 1), :] for s in range(4)]
            values.append(jnp.concatenate([rows[r // 2] for r in range(8)], axis=0))
        return block, lane, values

    def scatter(block, lane, values, i):
        at = jnp.tile(block, (8, 1)) == 8 * i + (iota((64, CELLS), 0) >> 3)
        twice = jnp.concatenate([lane, lane], axis=1)
        res = []
        for v in values:
            hi, lo = two(jnp.where(at, jnp.tile(v, (8, 1)), 0.0))
            res.append(dot_t(jnp.concatenate([hi, lo], axis=1), twice))
        return res, dot_t(jnp.where(at, 1.0, 0.0).astype(bf16), lane)

    here = receivers(self_v[2], HALO, obs_own)

    @pl.loop(0, HALF // 8)
    def _(i):
        res, cnt = scatter(*here, i)
        rows = pl.ds(pl.multiple_of(64 * i, 64), 64)
        heard[0, rows, :] = res[0]
        heard[1, rows, :] = res[1]
        count[rows, :] = cnt

    last = HALF // 8 - 1
    for side, base, i in ((0, HALO - BLOCKS, 0), (1, HALO + BLOCKS, last)):
        res, cnt = scatter(*receivers(near[side, 2], base, obs_near.at[side]), i)
        rows = slice(64 * i, 64 * i + 64)
        heard[0, rows, :] += res[0]
        heard[1, rows, :] += res[1]
        count[rows, :] += cnt

    for c in own_src:
        c.wait()
    bytes_of(stage.at[0:4 * BLOCKS, :], ex_send.at[0], ex_recv.at[0]).wait_recv()
    bytes_of(stage.at[0:16 * HALO, :], halo_send.at[0], halo_recv.at[0]).wait_recv()

    even_rows = iota((64, CELLS), 0) % 2 == 0
    keep_l = jnp.where(even_rows & (me == 0), 0.0, 1.0)
    keep_r = jnp.where(jnp.logical_not(even_rows) & (me == nm - 1), 0.0, 1.0)

    def kept(i, x):
        if isinstance(i, int):
            return x * keep_l if i == 0 else x * keep_r if i == last else x
        return x * jnp.where(i == 0, keep_l, jnp.where(i == last, keep_r, 1.0))

    def at64(i, first=0):
        return slice(first + 64 * i, first + 64 * i + 64) if isinstance(i, int) else pl.ds(
            pl.multiple_of(first + 64 * i, 8), 64)

    def put(b, p, i, x):
        b[p, at64(i, 8), :] = x
        hi, lo = two(x)
        lhs_hi[at64(2 * i + p), :] = hi
        lhs_lo[at64(2 * i + p), :] = lo

    def seams(b):
        top = iota((8, CELLS), 0) % 2 == 0
        for p in range(2):
            end = b[p, ROWS:ROWS + 8, :]
            start = b[p, 8:16, :]
            b[p, 0:8, :] = jnp.where(top, 0.0, pltpu.roll(end, 1, axis=0))
            b[p, ROWS + 8:ROWS + 16, :] = jnp.where(top, pltpu.roll(start, 7, axis=0), 0.0)

    @pl.loop(0, HALF // 8)
    def _(i):
        for p in range(2):
            x = jnp.concatenate(
                [stage[pl.ds(p * (4 * STAGE) + 8 * i + j, 8, stride=HALF), :] for j in range(8)], axis=0
            )
            x = kept(i, reorder(x) * dinv)
            q[0, p, at64(i), :] = x
            put(fwd_a, p, i, x)

    seams(fwd_a)

    own_table.wait()
    bytes_of(table.at[0:(nz - 1) * (NX - 1) * half_rows, :], fan_send.at[0], fan_recv.at[1]).wait_recv()
    to_scalars.wait()

    def pick_rows(first, source, lane):
        picked[pl.ds(first, 8), :] = jnp.concatenate(
            [table[pl.ds(index_s[source, lane + j], 1), :] for j in range(8)], axis=0
        )

    pick_rows(0, 0, BLOCKS - HALO)
    pick_rows(HALO + BLOCKS, 2, 0)

    for i in range(BLOCKS // 8):
        pick_rows(HALO + 8 * i, 1, 8 * i)

    swap = remote(picked, theirs, pick_send.at[0], pick_recv.at[0], c=other)
    swap.start()

    for z, x in far:
        m = z_at[z] + x_at[x]
        remote(slots.at[m], slots_in.at[me], sl_send.at[0], sl_recv.at[0], m=m).start()

    swap.wait_recv()
    wsig[...] = OMEGA * jnp.exp(reorder(jnp.where(choose[...] > 0.5, picked[...], theirs[...])))

    for i in range(HALF // 8):
        rows = []
        for j in range(8):
            a = jnp.broadcast_to(wsig[pl.ds(8 * i + j, 1), :], (8, CELLS))
            b = jnp.broadcast_to(wsig[pl.ds(HALF + 8 * i + j, 1), :], (8, CELLS))
            rows.append(jnp.where(odd == 0, a, b))
        cross[at64(i), :] = kept(i, jnp.concatenate(rows, axis=0) * dinv)

    lane_row = iota((1, CELLS), 1)
    ends = jnp.where((lane_row == 0) | (lane_row == CELLS // 2), CHAIN * dinv, 0.0)
    low_lane = iota((64, CELLS), 1) < CELLS // 4

    def sweep(old, new, qk, sign, weights):
        for first, until in GROUPS:
            rows = slice(128 * first, 128 * until)
            prod = dot(jnp.concatenate([lhs_hi[rows, :], lhs_lo[rows, :]], axis=1), weights[...])
            prod = prod[:, 0:CELLS] + prod[:, CELLS:]
            for i in range(first, until):
                turn = cross[at64(i), :]
                near_x = [old[p, 64 * i:64 * i + 80, :] for p in range(2)]
                for p in range(2):
                    k = 2 * (i - first) + p
                    end = jnp.where(low_lane, near_x[p][16:80], near_x[p][0:64])
                    both = turn * near_x[1 - p][8:72]
                    x = q[qk, p, at64(i), :] + ends * pltpu.roll(end, CELLS // 2, axis=1)
                    x = x + both if (sign > 0) == (p == 0) else x - both
                    x = x + prod[64 * k:64 * k + 64, :]
                    put(new, p, i, kept(i, x))
        seams(new)

    def sweeps(a, b, *args):
        sweep(a, b, *args)

        @pl.loop(0, ITERS // 2 - 1)
        def _(k):
            sweep(b, a, *args)
            sweep(a, b, *args)

    sweeps(fwd_a, fwd_b, 0, 1, wf)

    for i in range(HALF // 8):
        for p in range(2):
            x = count[at64(i), :] * fwd_b[p, at64(i, 8), :] - heard[p, at64(i), :]
            x = kept(i, x * dinv)
            q[1, p, at64(i), :] = x
            put(adj_a, p, i, x)

    seams(adj_a)

    sweeps(adj_a, adj_b, 1, -1, wa)

    for i in range(HALF // 8):
        psum_buf[at64(i), :] = (
            adj_b[0, at64(i, 8), :] * fwd_b[1, at64(i, 8), :]
            - adj_b[1, at64(i, 8), :] * fwd_b[0, at64(i, 8), :]
        )

    for i in range(BLOCKS // 16):
        for h in range(2):
            first = 8 * (8 * i + (HALO if h == 0 else 0)) + h
            acc = psum_buf[pl.ds(first, 8, stride=8), :]
            for s in range(1, 4):
                acc = acc + psum_buf[pl.ds(first + 2 * s, 8, stride=8), :]
            at = 8 * i + (HALF - HALO) * h
            part[at:at + 8, :] = acc * wsig[HALO + at:HALO + at + 8, :]

    hi, mid, lo = three(reorder(part[...]))
    sel = qmat[...]
    packed = dot(sel, hi) + dot(sel, mid) + dot(sel, lo)
    pack[...] = packed.reshape(nm, CAP, CELLS)

    takes = lax.rem(mx, 2) == core
    for z, x in far:
        m = z_at[z] + x_at[x]
        remote(
            pack.at[m], pack_in.at[core * nm + me], gp_send.at[0], gp_recv.at[0], m=m, c=lax.rem(x_at[x], 2)
        ).start()
    beside_me = remote(pack.at[me], pack_in.at[core * nm + me], gp_send.at[1], gp_recv.at[0], c=other)

    @pl.when(jnp.logical_not(takes))
    def _():
        beside_me.start()

    @pl.when(takes)
    def _():
        pack_in[core * nm + me] = pack[me]

    bytes_of(slots.at[0:nm - 1], sl_send.at[0], sl_recv.at[0]).wait_recv()
    slots_in[me] = slots[me]

    bytes_of(table.at[0:(nz - 1) * half_rows, :], ag_send.at[0], ag_recv.at[0]).wait_send()
    bytes_of(near, small_send.at[0], small_recv.at[0]).wait_send()
    bytes_of(stage.at[0:4 * BLOCKS, :], ex_send.at[0], ex_recv.at[0]).wait_send()
    obs_swap.wait_send()
    bytes_of(stage.at[0:16 * HALO, :], halo_send.at[0], halo_recv.at[0]).wait_send()
    bytes_of(obs_near, obs_send.at[0], obs_recv.at[0]).wait_send()
    bytes_of(table.at[0:nz * (NX - 1) * half_rows, :], fan_send.at[0], fan_recv.at[0]).wait_send()
    swap.wait_send()
    bytes_of(slots.at[0:nm - 1], sl_send.at[0], sl_recv.at[0]).wait_send()

    back = remote(total, total_in, to_send.at[0], to_recv.at[0], c=other)

    @pl.when(takes)
    def _():
        slot_in = slots_in[...].reshape(nm * CAP, CELLS)
        hit = jnp.where(slot_in == (iota((nm * CAP, CELLS), 1) + 1).astype(f32), 1.0, 0.0)
        hits[...] = hit.T.astype(bf16)

        bytes_of(pack_in.at[0:2 * nm - 1], gp_send.at[0], gp_recv.at[0]).wait_recv()
        rows = (pack_in[0:nm] + pack_in[nm:2 * nm]).reshape(nm * CAP, CELLS)
        hi, mid, lo = three(rows)
        sel = hits[0:OWNED, :]
        line[grp] = dot(sel, hi) + dot(sel, mid) + dot(sel, lo)

        for d in far_g:
            remote(line.at[grp], line.at[grp], ln_send.at[0], ln_recv.at[0], g=g_at[d]).start()
        bytes_of(line.at[0:ng - 1], ln_send.at[0], ln_recv.at[0]).wait_recv()
        summed = line[0]
        for g in range(1, ng):
            summed = summed + line[g]
        total[...] = summed
        back.start()
        out_ref[...] = summed
        bytes_of(line.at[0:ng - 1], ln_send.at[0], ln_recv.at[0]).wait_send()
        back.wait_send()

    @pl.when(jnp.logical_not(takes))
    def _():
        beside_me.wait_send()
        back.wait_recv()
        out_ref[...] = total_in[...]

    bytes_of(pack.at[0:nm - 1], gp_send.at[0], gp_recv.at[0]).wait_send()


def local(log_sigma, block_owner, block_slot, coupling, sources, rcv_cell, observed):
    nm, ng = lax.axis_size("mesh"), lax.axis_size("group")
    vmem, hbm, dma = pltpu.VMEM, pl.BlockSpec(memory_space=pl.ANY), pltpu.SemaphoreType.DMA
    inside = pl.BlockSpec(memory_space=pltpu.VMEM)
    nz = nm // NX
    return pl.pallas_call(
        functools.partial(kernel, ng, nm),
        out_shape=pltpu.VMEM((OWNED, CELLS), f32),
        in_specs=[hbm] * 7,
        out_specs=inside,
        scratch_shapes=[
            vmem((8 * STAGE, CELLS), f32),
            vmem((nm * OWNED // 2, CELLS), f32),
            vmem((2, 3, 1, BLOCKS), i32),
            vmem((3, 1, BLOCKS), i32),
            vmem((CELLS, CELLS), f32),
            vmem((2, S, CELLS), f32),
            vmem((2, 2, S, CELLS), f32),
            vmem((8, BLOCKS), i32),
            pltpu.SMEM((8, BLOCKS), i32),
            vmem((STAGE, CELLS), f32),
            vmem((STAGE, CELLS), f32),
            vmem((STAGE, CELLS), f32),
            vmem((2, ROWS + 16, CELLS), f32),
            vmem((2, ROWS + 16, CELLS), f32),
            vmem((2, ROWS + 16, CELLS), f32),
            vmem((2, ROWS + 16, CELLS), f32),
            vmem((2 * ROWS, CELLS), bf16),
            vmem((2 * ROWS, CELLS), bf16),
            vmem((2, 2, ROWS, CELLS), f32),
            vmem((ROWS, CELLS), f32),
            vmem((STAGE, CELLS), f32),
            vmem((CELLS, nm * CAP), bf16),
            vmem((2, ROWS, CELLS), f32),
            vmem((ROWS, CELLS), f32),
            vmem((2 * CELLS, 2 * CELLS), bf16),
            vmem((2 * CELLS, 2 * CELLS), bf16),
            vmem((nm * CAP, BLOCKS), bf16),
            vmem((ROWS, CELLS), f32),
            vmem((BLOCKS, CELLS), f32),
            vmem((nm, CAP, CELLS), f32),
            vmem((nm, CAP, CELLS), f32),
            vmem((nm, CAP, CELLS), f32),
            vmem((2 * nm, CAP, CELLS), f32),
            vmem((ng, OWNED, CELLS), f32),
            vmem((OWNED, CELLS), f32),
            vmem((OWNED, CELLS), f32),
            dma((10,)),
            dma((2,)), dma((2,)),
            dma((1,)), dma((1,)),
            dma((1,)), dma((1,)),
            dma((1,)), dma((1,)),
            dma((1,)), dma((nz,)),
            dma((1,)), dma((2,)),
            dma((1,)), dma((1,)),
            dma((1,)), dma((1,)),
            dma((2,)), dma((1,)),
            dma((1,)), dma((1,)),
            dma((1,)), dma((1,)),
            dma(()),
        ],
        compiler_params=pltpu.CompilerParams(collective_id=0, has_side_effects=True),
    )(
        block_owner.reshape(1, BLOCKS), block_slot, rcv_cell, observed.reshape(S, CELLS), coupling, log_sigma, sources.reshape(S, BLOCKS, CELLS)
    )


def solution(mesh):
    in_specs = (
        P("mesh", None),
        P("group", "mesh", None),
        P("group", "mesh"),
        P(),
        P("group", "comp", None, "mesh", None),
        P("group", "mesh"),
        P("group", "comp", None, "mesh"),
    )
    return jax.shard_map(local, mesh=mesh, in_specs=in_specs, out_specs=P("mesh", None), check_vma=False)
```

```python
import functools

import jax
import jax.numpy as jnp
from jax import lax
from jax.experimental import pallas as pl
from jax.experimental.pallas import tpu as pltpu
from jax.sharding import PartitionSpec as P

CELLS = 128
S = 8
ITERS = 6
CAP = 8
NX = 4
BLOCKS = 128
HALO = 8
HALF = (BLOCKS + 2 * HALO) // 2
ROWS = HALF * 8
STAGE = BLOCKS + 2 * HALO
OWNED = 64
GROUPS = ((0, 3), (3, 6), (6, 9))
OMEGA = 0.8
CHAIN = 1.0

f32, bf16, i32 = jnp.float32, jnp.bfloat16, jnp.int32
NT = (((1,), (1,)), ((), ()))


def iota(shape, dim):
    return lax.broadcasted_iota(i32, shape, dim)


def two(x):
    hi = x.astype(bf16)
    return hi, (x - hi.astype(f32)).astype(bf16)


def three(x):
    hi = x.astype(bf16)
    rest = x - hi.astype(f32)
    mid = rest.astype(bf16)
    return hi, mid, (rest - mid.astype(f32)).astype(bf16)


def dot(a, b):
    return jnp.dot(a, b, preferred_element_type=f32)


def dot_t(a, b):
    return lax.dot_general(a, b, NT, preferred_element_type=f32)


def cell_of(lane):
    return jnp.where(lane == CELLS // 2, CELLS - 1, jnp.where(lane == CELLS - 1, CELLS // 2, lane))


def reorder(x):
    lane = iota(x.shape, 1)
    up = pltpu.roll(x, CELLS // 2 + 1, axis=1)
    down = pltpu.roll(x, CELLS // 2 - 1, axis=1)
    return jnp.where(lane == CELLS // 2, up, jnp.where(lane == CELLS - 1, down, x))


def column(row):
    n = row.shape[1]
    return jnp.sum(jnp.where(iota((n, n), 0) == iota((n, n), 1), row, 0.0), axis=1, keepdims=True)


def kernel(
    ng, nm, own_ref, slot_ref, rcv_ref, obs_ref, cpl_ref, ls_ref, src_ref, out_ref,
    stage, table, near, self_v, cpl_v, obs_own, obs_near, index_v, index_s, picked, theirs, choose,
    fwd_a, fwd_b, adj_a, adj_b, lhs_hi, lhs_lo, q, cross, wsig, hits, heard, count, wf, wa, qmat, psum_buf, part,
    slots, slots_in, pack, pack_in, line, total, total_in,
    local_sem, ex_send, ex_recv, halo_send, halo_recv, obs_send, obs_recv, small_send, small_recv,
    ag_send, ag_recv, fan_send, fan_recv, pick_send, pick_recv, sl_send, sl_recv, gp_send, gp_recv,
    ln_send, ln_recv, to_send, to_recv, index_sem,
):
    me = lax.axis_index("mesh")
    core = lax.axis_index("comp")
    grp = lax.axis_index("group")
    other = 1 - core
    nz = nm // NX
    mz, mx = lax.div(me, NX), lax.rem(me, NX)
    z_at = [lax.rem(mz + d, nz) * NX for d in range(nz)]
    x_at = [lax.rem(mx + d, NX) for d in range(NX)]
    g_at = [lax.rem(grp + d, ng) for d in range(ng)]
    right, left = lax.rem(me + 1, nm), lax.rem(me + nm - 1, nm)

    def ring(d, n):
        return min(d, n - d)

    far_z, far_x, far_g = (sorted(range(1, n), key=lambda d: -ring(d, n)) for n in (nz, NX, ng))
    far = sorted(
        [(z, x) for z in range(nz) for x in range(NX) if z or x], key=lambda d: -ring(d[0], nz) - ring(d[1], NX)
    )

    def remote(src, dst, ssem, rsem, g=None, m=None, c=None):
        where = (grp if g is None else g, me if m is None else m, core if c is None else c)
        return pltpu.make_async_remote_copy(
            src_ref=src, dst_ref=dst, send_sem=ssem, recv_sem=rsem,
            device_id=where, device_id_type=pl.DeviceIdType.MESH,
        )

    def bytes_of(ref, ssem, rsem):
        return remote(ref, ref, ssem, rsem, c=other)

    barrier = pltpu.get_barrier_semaphore()

    def greet(g=None, m=None, c=None):
        where = (grp if g is None else g, me if m is None else m, core if c is None else c)
        pl.semaphore_signal(barrier, inc=1, device_id=where, device_id_type=pl.DeviceIdType.MESH)

    for z in far_z:
        greet(m=z_at[z] + mx)
    for d in far_g:
        greet(g=g_at[d])
    for x in far_x:
        greet(m=z_at[0] + x_at[x])
    for m in (left, right):
        for c in (core, other):
            greet(m=m, c=c)
    greet(c=other)

    half_rows = OWNED // 2
    own_half = pl.ds(pl.multiple_of(core * half_rows, 8), half_rows)

    def table_rows(owner):
        return table.at[pl.ds(pl.multiple_of(owner * half_rows, 8), half_rows), :]

    def stage_rows(p, s, first, n):
        return stage.at[pl.ds(pl.multiple_of(p * (4 * STAGE) + s * STAGE + first, 8), n), :]

    own_table = pltpu.make_async_copy(ls_ref.at[own_half, :], table_rows(me), local_sem.at[1])
    own_table.start()
    own_src = [
        pltpu.make_async_copy(src_ref.at[4 * core + s], stage_rows(core, s, HALO, BLOCKS), local_sem.at[s + 2])
        for s in range(4)
    ]
    own_cells = [
        pltpu.make_async_copy(ref, self_v.at[k], local_sem.at[6 + k])
        for k, ref in enumerate((own_ref, slot_ref, rcv_ref))
    ]
    own_cpl = pltpu.make_async_copy(cpl_ref, cpl_v, local_sem.at[9])
    own_obs = pltpu.make_async_copy(obs_ref, obs_own.at[core], local_sem.at[0])
    for c in [own_cpl, own_obs] + own_cells + own_src:
        c.start()

    pl.semaphore_wait(barrier, nz - 1 + NX - 1 + ng - 1 + 5)

    for z in far_z[::-1]:
        remote(ls_ref.at[own_half, :], table_rows(me), ag_send.at[0], ag_recv.at[mz], m=z_at[z] + mx).start()

    for x in far_x:
        remote(
            ls_ref.at[own_half, :], table_rows(me), fan_send.at[0], fan_recv.at[0], m=z_at[0] + x_at[x]
        ).start()

    for side, m in ((0, right), (1, left)):
        for k, ref in enumerate((own_ref, slot_ref, rcv_ref)):
            remote(ref, near.at[side, k], small_send.at[0], small_recv.at[0], m=m).start()
    for s in range(4):
        remote(
            src_ref.at[4 * other + s], stage_rows(core, s, HALO, BLOCKS), ex_send.at[0], ex_recv.at[0], c=other
        ).start()
    obs_swap = remote(obs_ref, obs_own.at[core], ex_send.at[1], ex_recv.at[1], c=other)
    obs_swap.start()
    for side, m, first, into in ((0, right, BLOCKS - HALO, 0), (1, left, 0, STAGE - HALO)):
        for c in range(2):
            for s in range(4):
                remote(
                    src_ref.at[4 * c + s, pl.ds(first, HALO), :], stage_rows(core, s, into, HALO),
                    halo_send.at[0], halo_recv.at[0], m=m, c=c,
                ).start()
            remote(obs_ref, obs_near.at[side, core], obs_send.at[0], obs_recv.at[0], m=m, c=c).start()

    eye = iota((CELLS, CELLS), 0) == iota((CELLS, CELLS), 1)
    square = (CELLS, CELLS)
    beside = jnp.abs(cell_of(iota(square, 0)) - cell_of(iota(square, 1))) == 1
    own_cpl.wait()
    cpl_v[...] = reorder(cpl_v[...])
    mid_row, last_row = cpl_v[CELLS // 2:CELLS // 2 + 1, :], cpl_v[CELLS - 1:, :]
    cpl_v[CELLS // 2:CELLS // 2 + 1, :] = last_row
    cpl_v[CELLS - 1:, :] = mid_row
    cpl = cpl_v[...]
    dinv = 1.0 / jnp.sum(jnp.where(eye, cpl, 0.0), axis=0, keepdims=True)
    for m, w in ((cpl.T, wf), (cpl, wa)):
        scaled = -dinv * (jnp.where(eye, 0.0, m) - jnp.where(beside, CHAIN, 0.0))
        hi, lo = two(scaled)
        w[0:CELLS, 0:CELLS] = hi
        w[0:CELLS, CELLS:] = lo
        w[CELLS:, 0:CELLS] = hi
        w[CELLS:, CELLS:] = lo

    for c in own_cells:
        c.wait()
    owner_row = self_v[0]
    slot_row = self_v[1]
    owner_col = column(owner_row.astype(f32)).astype(i32)
    earlier = (owner_col == owner_row) & (iota((BLOCKS, BLOCKS), 0) < iota((BLOCKS, BLOCKS), 1))
    rank = jnp.sum(jnp.where(earlier, 1.0, 0.0), axis=0, keepdims=True).astype(i32)
    place = owner_row * CAP + rank
    pick = jnp.where(iota((nm * CAP, BLOCKS), 0) == place, 1.0, 0.0)
    qmat[...] = pick.astype(bf16)
    slot_of = jnp.sum(pick * (slot_row + 1).astype(f32), axis=1, keepdims=True)
    slots[...] = jnp.broadcast_to(slot_of, (nm * CAP, CELLS)).reshape(nm, CAP, CELLS)

    def relay(owner, k, m):
        remote(table_rows(owner), table_rows(owner), fan_send.at[0], fan_recv.at[k], m=m).start()

    def along_z(z):
        owner = z_at[z] + mx
        remote(
            table_rows(owner), table_rows(owner), ag_send.at[0], ag_recv.at[lax.div(z_at[z], NX)], c=other
        ).wait_recv()
        return owner

    near_z = far_z[1:][::-1]
    for z in near_z[:2]:
        owner = along_z(z)
        for x in far_x:
            relay(owner, 1, z_at[0] + x_at[x])
    bytes_of(table.at[0:(NX - 1) * half_rows, :], fan_send.at[0], fan_recv.at[0]).wait_recv()
    for x in far_x[::-1]:
        relay(z_at[0] + x_at[x], 1, z_at[far_z[0]] + mx)
    for z in near_z[2:]:
        owner = along_z(z)
        for x in far_x:
            relay(owner, 1, z_at[0] + x_at[x])
    along_z(far_z[0])

    bytes_of(near, small_send.at[0], small_recv.at[0]).wait_recv()
    own3 = jnp.concatenate([near[0, 0], owner_row, near[1, 0]] + [owner_row] * 5, axis=0)
    slot3 = jnp.concatenate([near[0, 1], slot_row, near[1, 1]] + [slot_row] * 5, axis=0)
    index_v[...] = own3 * half_rows + (slot3 & (half_rows - 1))
    to_scalars = pltpu.make_async_copy(index_v, index_s, index_sem)
    to_scalars.start()

    mine = jnp.where((slot3 >> 5) == core, 1.0, 0.0)
    wide = (HALO, BLOCKS)
    col_l = jnp.sum(jnp.where(iota(wide, 0) + BLOCKS - HALO == iota(wide, 1), mine[0:1], 0.0), axis=1, keepdims=True)
    col_r = jnp.sum(jnp.where(iota(wide, 0) == iota(wide, 1), mine[2:3], 0.0), axis=1, keepdims=True)
    choose[0:HALO, :] = jnp.broadcast_to(col_l, (HALO, CELLS))
    choose[HALO:HALO + BLOCKS, :] = jnp.broadcast_to(column(mine[1:2]), (BLOCKS, CELLS))
    choose[HALO + BLOCKS:, :] = jnp.broadcast_to(col_r, (HALO, CELLS))

    own_obs.wait()
    obs_swap.wait_recv()
    bytes_of(obs_near, obs_send.at[0], obs_recv.at[0]).wait_recv()
    odd = iota((8, CELLS), 0) % 2

    def receivers(cells, base, obs_at):
        block = (cells >> 7) + base - HALF * odd
        lane = jnp.where(cell_of(iota(square, 0)) == (cells & (CELLS - 1)), 1.0, 0.0).astype(bf16)
        values = []
        for p in range(2):
            rows = [obs_at[p, pl.ds(4 * core + s, 1), :] for s in range(4)]
            values.append(jnp.concatenate([rows[r // 2] for r in range(8)], axis=0))
        return block, lane, values

    def scatter(block, lane, values, i):
        at = jnp.tile(block, (8, 1)) == 8 * i + (iota((64, CELLS), 0) >> 3)
        twice = jnp.concatenate([lane, lane], axis=1)
        res = []
        for v in values:
            hi, lo = two(jnp.where(at, jnp.tile(v, (8, 1)), 0.0))
            res.append(dot_t(jnp.concatenate([hi, lo], axis=1), twice))
        return res, dot_t(jnp.where(at, 1.0, 0.0).astype(bf16), lane)

    here = receivers(self_v[2], HALO, obs_own)

    @pl.loop(0, HALF // 8)
    def _(i):
        res, cnt = scatter(*here, i)
        rows = pl.ds(pl.multiple_of(64 * i, 64), 64)
        heard[0, rows, :] = res[0]
        heard[1, rows, :] = res[1]
        count[rows, :] = cnt

    last = HALF // 8 - 1
    for side, base, i in ((0, HALO - BLOCKS, 0), (1, HALO + BLOCKS, last)):
        res, cnt = scatter(*receivers(near[side, 2], base, obs_near.at[side]), i)
        rows = slice(64 * i, 64 * i + 64)
        heard[0, rows, :] += res[0]
        heard[1, rows, :] += res[1]
        count[rows, :] += cnt

    for c in own_src:
        c.wait()
    bytes_of(stage.at[0:4 * BLOCKS, :], ex_send.at[0], ex_recv.at[0]).wait_recv()
    bytes_of(stage.at[0:16 * HALO, :], halo_send.at[0], halo_recv.at[0]).wait_recv()

    even_rows = iota((64, CELLS), 0) % 2 == 0
    keep_l = jnp.where(even_rows & (me == 0), 0.0, 1.0)
    keep_r = jnp.where(jnp.logical_not(even_rows) & (me == nm - 1), 0.0, 1.0)

    def kept(i, x):
        if isinstance(i, int):
            return x * keep_l if i == 0 else x * keep_r if i == last else x
        return x * jnp.where(i == 0, keep_l, jnp.where(i == last, keep_r, 1.0))

    def at64(i, first=0):
        return slice(first + 64 * i, first + 64 * i + 64) if isinstance(i, int) else pl.ds(
            pl.multiple_of(first + 64 * i, 8), 64)

    def put(b, p, i, x):
        b[p, at64(i, 8), :] = x
        hi, lo = two(x)
        lhs_hi[at64(2 * i + p), :] = hi
        lhs_lo[at64(2 * i + p), :] = lo

    def seams(b):
        top = iota((8, CELLS), 0) % 2 == 0
        for p in range(2):
            end = b[p, ROWS:ROWS + 8, :]
            start = b[p, 8:16, :]
            b[p, 0:8, :] = jnp.where(top, 0.0, pltpu.roll(end, 1, axis=0))
            b[p, ROWS + 8:ROWS + 16, :] = jnp.where(top, pltpu.roll(start, 7, axis=0), 0.0)

    @pl.loop(0, HALF // 8)
    def _(i):
        for p in range(2):
            x = jnp.concatenate(
                [stage[pl.ds(p * (4 * STAGE) + 8 * i + j, 8, stride=HALF), :] for j in range(8)], axis=0
            )
            x = kept(i, reorder(x) * dinv)
            q[0, p, at64(i), :] = x
            put(fwd_a, p, i, x)

    seams(fwd_a)

    own_table.wait()
    bytes_of(table.at[0:(nz - 1) * (NX - 1) * half_rows, :], fan_send.at[0], fan_recv.at[1]).wait_recv()
    to_scalars.wait()

    def pick_rows(first, source, lane):
        picked[pl.ds(first, 8), :] = jnp.concatenate(
            [table[pl.ds(index_s[source, lane + j], 1), :] for j in range(8)], axis=0
        )

    pick_rows(0, 0, BLOCKS - HALO)
    pick_rows(HALO + BLOCKS, 2, 0)

    for i in range(BLOCKS // 8):
        pick_rows(HALO + 8 * i, 1, 8 * i)

    swap = remote(picked, theirs, pick_send.at[0], pick_recv.at[0], c=other)
    swap.start()

    for z, x in far:
        m = z_at[z] + x_at[x]
        remote(slots.at[m], slots_in.at[me], sl_send.at[0], sl_recv.at[0], m=m).start()

    swap.wait_recv()
    wsig[...] = OMEGA * jnp.exp(reorder(jnp.where(choose[...] > 0.5, picked[...], theirs[...])))

    for i in range(HALF // 8):
        rows = []
        for j in range(8):
            a = jnp.broadcast_to(wsig[pl.ds(8 * i + j, 1), :], (8, CELLS))
            b = jnp.broadcast_to(wsig[pl.ds(HALF + 8 * i + j, 1), :], (8, CELLS))
            rows.append(jnp.where(odd == 0, a, b))
        cross[at64(i), :] = kept(i, jnp.concatenate(rows, axis=0) * dinv)

    lane_row = iota((1, CELLS), 1)
    ends = jnp.where((lane_row == 0) | (lane_row == CELLS // 2), CHAIN * dinv, 0.0)
    low_lane = iota((64, CELLS), 1) < CELLS // 4

    def sweep(old, new, qk, sign, weights):
        for first, until in GROUPS:
            rows = slice(128 * first, 128 * until)
            prod = dot(jnp.concatenate([lhs_hi[rows, :], lhs_lo[rows, :]], axis=1), weights[...])
            prod = prod[:, 0:CELLS] + prod[:, CELLS:]
            for i in range(first, until):
                turn = cross[at64(i), :]
                near_x = [old[p, 64 * i:64 * i + 80, :] for p in range(2)]
                for p in range(2):
                    k = 2 * (i - first) + p
                    end = jnp.where(low_lane, near_x[p][16:80], near_x[p][0:64])
                    both = turn * near_x[1 - p][8:72]
                    x = q[qk, p, at64(i), :] + ends * pltpu.roll(end, CELLS // 2, axis=1)
                    x = x + both if (sign > 0) == (p == 0) else x - both
                    x = x + prod[64 * k:64 * k + 64, :]
                    put(new, p, i, kept(i, x))
        seams(new)

    def sweeps(a, b, *args):
        sweep(a, b, *args)

        @pl.loop(0, ITERS // 2 - 1)
        def _(k):
            sweep(b, a, *args)
            sweep(a, b, *args)

    sweeps(fwd_a, fwd_b, 0, 1, wf)

    for i in range(HALF // 8):
        for p in range(2):
            x = count[at64(i), :] * fwd_b[p, at64(i, 8), :] - heard[p, at64(i), :]
            x = kept(i, x * dinv)
            q[1, p, at64(i), :] = x
            put(adj_a, p, i, x)

    seams(adj_a)

    sweeps(adj_a, adj_b, 1, -1, wa)

    for i in range(HALF // 8):
        psum_buf[at64(i), :] = (
            adj_b[0, at64(i, 8), :] * fwd_b[1, at64(i, 8), :]
            - adj_b[1, at64(i, 8), :] * fwd_b[0, at64(i, 8), :]
        )

    for i in range(BLOCKS // 16):
        for h in range(2):
            first = 8 * (8 * i + (HALO if h == 0 else 0)) + h
            acc = psum_buf[pl.ds(first, 8, stride=8), :]
            for s in range(1, 4):
                acc = acc + psum_buf[pl.ds(first + 2 * s, 8, stride=8), :]
            at = 8 * i + (HALF - HALO) * h
            part[at:at + 8, :] = acc * wsig[HALO + at:HALO + at + 8, :]

    hi, mid, lo = three(reorder(part[...]))
    sel = qmat[...]
    packed = dot(sel, hi) + dot(sel, mid) + dot(sel, lo)
    pack[...] = packed.reshape(nm, CAP, CELLS)

    takes = lax.rem(mx + 1, 2) == core
    for z, x in far:
        m = z_at[z] + x_at[x]
        remote(
            pack.at[m], pack_in.at[core * nm + me], gp_send.at[0], gp_recv.at[0], m=m, c=lax.rem(x_at[x] + 1, 2)
        ).start()
    beside_me = remote(pack.at[me], pack_in.at[core * nm + me], gp_send.at[1], gp_recv.at[0], c=other)

    @pl.when(jnp.logical_not(takes))
    def _():
        beside_me.start()

    @pl.when(takes)
    def _():
        pack_in[core * nm + me] = pack[me]

    bytes_of(slots.at[0:nm - 1], sl_send.at[0], sl_recv.at[0]).wait_recv()
    slots_in[me] = slots[me]

    bytes_of(table.at[0:(nz - 1) * half_rows, :], ag_send.at[0], ag_recv.at[0]).wait_send()
    bytes_of(near, small_send.at[0], small_recv.at[0]).wait_send()
    bytes_of(stage.at[0:4 * BLOCKS, :], ex_send.at[0], ex_recv.at[0]).wait_send()
    obs_swap.wait_send()
    bytes_of(stage.at[0:16 * HALO, :], halo_send.at[0], halo_recv.at[0]).wait_send()
    bytes_of(obs_near, obs_send.at[0], obs_recv.at[0]).wait_send()
    bytes_of(table.at[0:nz * (NX - 1) * half_rows, :], fan_send.at[0], fan_recv.at[0]).wait_send()
    swap.wait_send()
    bytes_of(slots.at[0:nm - 1], sl_send.at[0], sl_recv.at[0]).wait_send()

    back = remote(total, total_in, to_send.at[0], to_recv.at[0], c=other)

    @pl.when(takes)
    def _():
        slot_in = slots_in[...].reshape(nm * CAP, CELLS)
        hit = jnp.where(slot_in == (iota((nm * CAP, CELLS), 1) + 1).astype(f32), 1.0, 0.0)
        hits[...] = hit.T.astype(bf16)

        bytes_of(pack_in.at[0:2 * nm - 1], gp_send.at[0], gp_recv.at[0]).wait_recv()
        rows = (pack_in[0:nm] + pack_in[nm:2 * nm]).reshape(nm * CAP, CELLS)
        hi, mid, lo = three(rows)
        sel = hits[0:OWNED, :]
        line[grp] = dot(sel, hi) + dot(sel, mid) + dot(sel, lo)

        for d in far_g:
            remote(line.at[grp], line.at[grp], ln_send.at[0], ln_recv.at[0], g=g_at[d]).start()
        bytes_of(line.at[0:ng - 1], ln_send.at[0], ln_recv.at[0]).wait_recv()
        summed = line[0]
        for g in range(1, ng):
            summed = summed + line[g]
        total[...] = summed
        back.start()
        out_ref[...] = summed
        bytes_of(line.at[0:ng - 1], ln_send.at[0], ln_recv.at[0]).wait_send()
        back.wait_send()

    @pl.when(jnp.logical_not(takes))
    def _():
        beside_me.wait_send()
        back.wait_recv()
        out_ref[...] = total_in[...]

    bytes_of(pack.at[0:nm - 1], gp_send.at[0], gp_recv.at[0]).wait_send()


def local(log_sigma, block_owner, block_slot, coupling, sources, rcv_cell, observed):
    nm, ng = lax.axis_size("mesh"), lax.axis_size("group")
    vmem, hbm, dma = pltpu.VMEM, pl.BlockSpec(memory_space=pl.ANY), pltpu.SemaphoreType.DMA
    inside = pl.BlockSpec(memory_space=pltpu.VMEM)
    nz = nm // NX
    return pl.pallas_call(
        functools.partial(kernel, ng, nm),
        out_shape=pltpu.VMEM((OWNED, CELLS), f32),
        in_specs=[hbm] * 7,
        out_specs=inside,
        scratch_shapes=[
            vmem((8 * STAGE, CELLS), f32),
            vmem((nm * OWNED // 2, CELLS), f32),
            vmem((2, 3, 1, BLOCKS), i32),
            vmem((3, 1, BLOCKS), i32),
            vmem((CELLS, CELLS), f32),
            vmem((2, S, CELLS), f32),
            vmem((2, 2, S, CELLS), f32),
            vmem((8, BLOCKS), i32),
            pltpu.SMEM((8, BLOCKS), i32),
            vmem((STAGE, CELLS), f32),
            vmem((STAGE, CELLS), f32),
            vmem((STAGE, CELLS), f32),
            vmem((2, ROWS + 16, CELLS), f32),
            vmem((2, ROWS + 16, CELLS), f32),
            vmem((2, ROWS + 16, CELLS), f32),
            vmem((2, ROWS + 16, CELLS), f32),
            vmem((2 * ROWS, CELLS), bf16),
            vmem((2 * ROWS, CELLS), bf16),
            vmem((2, 2, ROWS, CELLS), f32),
            vmem((ROWS, CELLS), f32),
            vmem((STAGE, CELLS), f32),
            vmem((CELLS, nm * CAP), bf16),
            vmem((2, ROWS, CELLS), f32),
            vmem((ROWS, CELLS), f32),
            vmem((2 * CELLS, 2 * CELLS), bf16),
            vmem((2 * CELLS, 2 * CELLS), bf16),
            vmem((nm * CAP, BLOCKS), bf16),
            vmem((ROWS, CELLS), f32),
            vmem((BLOCKS, CELLS), f32),
            vmem((nm, CAP, CELLS), f32),
            vmem((nm, CAP, CELLS), f32),
            vmem((nm, CAP, CELLS), f32),
            vmem((2 * nm, CAP, CELLS), f32),
            vmem((ng, OWNED, CELLS), f32),
            vmem((OWNED, CELLS), f32),
            vmem((OWNED, CELLS), f32),
            dma((10,)),
            dma((2,)), dma((2,)),
            dma((1,)), dma((1,)),
            dma((1,)), dma((1,)),
            dma((1,)), dma((1,)),
            dma((1,)), dma((nz,)),
            dma((1,)), dma((2,)),
            dma((1,)), dma((1,)),
            dma((1,)), dma((1,)),
            dma((2,)), dma((1,)),
            dma((1,)), dma((1,)),
            dma((1,)), dma((1,)),
            dma(()),
        ],
        compiler_params=pltpu.CompilerParams(collective_id=0, has_side_effects=True),
    )(
        block_owner.reshape(1, BLOCKS), block_slot, rcv_cell, observed.reshape(S, CELLS), coupling, log_sigma, sources.reshape(S, BLOCKS, CELLS)
    )


def solution(mesh):
    in_specs = (
        P("mesh", None),
        P("group", "mesh", None),
        P("group", "mesh"),
        P(),
        P("group", "comp", None, "mesh", None),
        P("group", "mesh"),
        P("group", "comp", None, "mesh"),
    )
    return jax.shard_map(local, mesh=mesh, in_specs=in_specs, out_specs=P("mesh", None), check_vma=False)
```

```python
import functools

import jax
import jax.numpy as jnp
from jax import lax
from jax.experimental import pallas as pl
from jax.experimental.pallas import tpu as pltpu
from jax.sharding import PartitionSpec as P

CELLS = 128
S = 8
ITERS = 6
CAP = 8
NX = 4
BLOCKS = 128
HALO = 8
HALF = (BLOCKS + 2 * HALO) // 2
ROWS = HALF * 8
STAGE = BLOCKS + 2 * HALO
OWNED = 64
GROUPS = ((0, 3), (3, 6), (6, 9))
OMEGA = 0.8
CHAIN = 1.0

f32, bf16, i32 = jnp.float32, jnp.bfloat16, jnp.int32
NT = (((1,), (1,)), ((), ()))


def iota(shape, dim):
    return lax.broadcasted_iota(i32, shape, dim)


def two(x):
    hi = x.astype(bf16)
    return hi, (x - hi.astype(f32)).astype(bf16)


def three(x):
    hi = x.astype(bf16)
    rest = x - hi.astype(f32)
    mid = rest.astype(bf16)
    return hi, mid, (rest - mid.astype(f32)).astype(bf16)


def dot(a, b):
    return jnp.dot(a, b, preferred_element_type=f32)


def dot_t(a, b):
    return lax.dot_general(a, b, NT, preferred_element_type=f32)


def cell_of(lane):
    return jnp.where(lane == CELLS // 2, CELLS - 1, jnp.where(lane == CELLS - 1, CELLS // 2, lane))


def reorder(x):
    lane = iota(x.shape, 1)
    up = pltpu.roll(x, CELLS // 2 + 1, axis=1)
    down = pltpu.roll(x, CELLS // 2 - 1, axis=1)
    return jnp.where(lane == CELLS // 2, up, jnp.where(lane == CELLS - 1, down, x))


def column(row):
    n = row.shape[1]
    return jnp.sum(jnp.where(iota((n, n), 0) == iota((n, n), 1), row, 0.0), axis=1, keepdims=True)


def kernel(
    ng, nm, own_ref, slot_ref, rcv_ref, obs_ref, cpl_ref, ls_ref, src_ref, out_ref,
    stage, table, near, self_v, cpl_v, obs_own, obs_near, index_v, index_s, picked, theirs, choose,
    fwd_a, fwd_b, adj_a, adj_b, lhs_hi, lhs_lo, q, cross, wsig, hits, heard, count, wf, wa, qmat, psum_buf, part,
    slots, slots_in, pack, pack_in, line, total, total_in,
    local_sem, ex_send, ex_recv, halo_send, halo_recv, obs_send, obs_recv, small_send, small_recv,
    ag_send, ag_recv, fan_send, fan_recv, pick_send, pick_recv, sl_send, sl_recv, gp_send, gp_recv,
    ln_send, ln_recv, to_send, to_recv, index_sem,
):
    me = lax.axis_index("mesh")
    core = lax.axis_index("comp")
    grp = lax.axis_index("group")
    other = 1 - core
    nz = nm // NX
    mz, mx = lax.div(me, NX), lax.rem(me, NX)
    z_at = [lax.rem(mz + d, nz) * NX for d in range(nz)]
    x_at = [lax.rem(mx + d, NX) for d in range(NX)]
    g_at = [lax.rem(grp + d, ng) for d in range(ng)]
    right, left = lax.rem(me + 1, nm), lax.rem(me + nm - 1, nm)

    def ring(d, n):
        return min(d, n - d)

    far_z, far_x, far_g = (sorted(range(1, n), key=lambda d: -ring(d, n)) for n in (nz, NX, ng))
    far = sorted(
        [(z, x) for z in range(nz) for x in range(NX) if z or x], key=lambda d: -ring(d[0], nz) - ring(d[1], NX)
    )

    def remote(src, dst, ssem, rsem, g=None, m=None, c=None):
        where = (grp if g is None else g, me if m is None else m, core if c is None else c)
        return pltpu.make_async_remote_copy(
            src_ref=src, dst_ref=dst, send_sem=ssem, recv_sem=rsem,
            device_id=where, device_id_type=pl.DeviceIdType.MESH,
        )

    def bytes_of(ref, ssem, rsem):
        return remote(ref, ref, ssem, rsem, c=other)

    barrier = pltpu.get_barrier_semaphore()

    def greet(g=None, m=None, c=None):
        where = (grp if g is None else g, me if m is None else m, core if c is None else c)
        pl.semaphore_signal(barrier, inc=1, device_id=where, device_id_type=pl.DeviceIdType.MESH)

    for z in far_z:
        greet(m=z_at[z] + mx)
    for d in far_g:
        greet(g=g_at[d])
    for x in far_x:
        greet(m=z_at[0] + x_at[x])
    for m in (left, right):
        for c in (core, other):
            greet(m=m, c=c)
    greet(c=other)

    half_rows = OWNED // 2
    own_half = pl.ds(pl.multiple_of(core * half_rows, 8), half_rows)

    def table_rows(owner):
        return table.at[pl.ds(pl.multiple_of(owner * half_rows, 8), half_rows), :]

    def stage_rows(p, s, first, n):
        return stage.at[pl.ds(pl.multiple_of(p * (4 * STAGE) + s * STAGE + first, 8), n), :]

    own_table = pltpu.make_async_copy(ls_ref.at[own_half, :], table_rows(me), local_sem.at[1])
    own_table.start()
    own_src = [
        pltpu.make_async_copy(src_ref.at[4 * core + s], stage_rows(core, s, HALO, BLOCKS), local_sem.at[s + 2])
        for s in range(4)
    ]
    own_cells = [
        pltpu.make_async_copy(ref, self_v.at[k], local_sem.at[6 + k])
        for k, ref in enumerate((own_ref, slot_ref, rcv_ref))
    ]
    own_cpl = pltpu.make_async_copy(cpl_ref, cpl_v, local_sem.at[9])
    own_obs = pltpu.make_async_copy(obs_ref, obs_own.at[core], local_sem.at[0])
    for c in [own_cpl, own_obs] + own_cells + own_src:
        c.start()

    pl.semaphore_wait(barrier, nz - 1 + NX - 1 + ng - 1 + 5)

    for z in far_z[::-1]:
        remote(ls_ref.at[own_half, :], table_rows(me), ag_send.at[0], ag_recv.at[mz], m=z_at[z] + mx).start()

    for x in far_x:
        remote(
            ls_ref.at[own_half, :], table_rows(me), fan_send.at[0], fan_recv.at[0], m=z_at[0] + x_at[x]
        ).start()

    for side, m in ((0, right), (1, left)):
        for k, ref in enumerate((own_ref, slot_ref, rcv_ref)):
            remote(ref, near.at[side, k], small_send.at[0], small_recv.at[0], m=m).start()
    for s in range(4):
        remote(
            src_ref.at[4 * other + s], stage_rows(core, s, HALO, BLOCKS), ex_send.at[0], ex_recv.at[0], c=other
        ).start()
    obs_swap = remote(obs_ref, obs_own.at[core], ex_send.at[1], ex_recv.at[1], c=other)
    obs_swap.start()
    for side, m, first, into in ((0, right, BLOCKS - HALO, 0), (1, left, 0, STAGE - HALO)):
        for c in range(2):
            for s in range(4):
                remote(
                    src_ref.at[4 * c + s, pl.ds(first, HALO), :], stage_rows(core, s, into, HALO),
                    halo_send.at[0], halo_recv.at[0], m=m, c=c,
                ).start()
            remote(obs_ref, obs_near.at[side, core], obs_send.at[0], obs_recv.at[0], m=m, c=c).start()

    eye = iota((CELLS, CELLS), 0) == iota((CELLS, CELLS), 1)
    square = (CELLS, CELLS)
    beside = jnp.abs(cell_of(iota(square, 0)) - cell_of(iota(square, 1))) == 1
    own_cpl.wait()
    cpl_v[...] = reorder(cpl_v[...])
    mid_row, last_row = cpl_v[CELLS // 2:CELLS // 2 + 1, :], cpl_v[CELLS - 1:, :]
    cpl_v[CELLS // 2:CELLS // 2 + 1, :] = last_row
    cpl_v[CELLS - 1:, :] = mid_row
    cpl = cpl_v[...]
    dinv = 1.0 / jnp.sum(jnp.where(eye, cpl, 0.0), axis=0, keepdims=True)
    for m, w in ((cpl.T, wf), (cpl, wa)):
        scaled = -dinv * (jnp.where(eye, 0.0, m) - jnp.where(beside, CHAIN, 0.0))
        hi, lo = two(scaled)
        w[0:CELLS, 0:CELLS] = hi
        w[0:CELLS, CELLS:] = lo
        w[CELLS:, 0:CELLS] = hi
        w[CELLS:, CELLS:] = lo

    for c in own_cells:
        c.wait()
    owner_row = self_v[0]
    slot_row = self_v[1]
    owner_col = column(owner_row.astype(f32)).astype(i32)
    earlier = (owner_col == owner_row) & (iota((BLOCKS, BLOCKS), 0) < iota((BLOCKS, BLOCKS), 1))
    rank = jnp.sum(jnp.where(earlier, 1.0, 0.0), axis=0, keepdims=True).astype(i32)
    place = owner_row * CAP + rank
    pick = jnp.where(iota((nm * CAP, BLOCKS), 0) == place, 1.0, 0.0)
    qmat[...] = pick.astype(bf16)
    slot_of = jnp.sum(pick * (slot_row + 1).astype(f32), axis=1, keepdims=True)
    slots[...] = jnp.broadcast_to(slot_of, (nm * CAP, CELLS)).reshape(nm, CAP, CELLS)

    def relay(owner, k, m):
        remote(table_rows(owner), table_rows(owner), fan_send.at[0], fan_recv.at[k], m=m).start()

    def along_z(z):
        owner = z_at[z] + mx
        remote(
            table_rows(owner), table_rows(owner), ag_send.at[0], ag_recv.at[lax.div(z_at[z], NX)], c=other
        ).wait_recv()
        return owner

    near_z = far_z[1:][::-1]
    for z in near_z[:2]:
        owner = along_z(z)
        for x in far_x:
            relay(owner, 1, z_at[0] + x_at[x])
    bytes_of(table.at[0:(NX - 1) * half_rows, :], fan_send.at[0], fan_recv.at[0]).wait_recv()
    for x in far_x[::-1]:
        relay(z_at[0] + x_at[x], 1, z_at[far_z[0]] + mx)
    for z in near_z[2:]:
        owner = along_z(z)
        for x in far_x:
            relay(owner, 1, z_at[0] + x_at[x])
    along_z(far_z[0])

    bytes_of(near, small_send.at[0], small_recv.at[0]).wait_recv()
    own3 = jnp.concatenate([near[0, 0], owner_row, near[1, 0]] + [owner_row] * 5, axis=0)
    slot3 = jnp.concatenate([near[0, 1], slot_row, near[1, 1]] + [slot_row] * 5, axis=0)
    index_v[...] = own3 * half_rows + (slot3 & (half_rows - 1))
    to_scalars = pltpu.make_async_copy(index_v, index_s, index_sem)
    to_scalars.start()

    mine = jnp.where((slot3 >> 5) == core, 1.0, 0.0)
    wide = (HALO, BLOCKS)
    col_l = jnp.sum(jnp.where(iota(wide, 0) + BLOCKS - HALO == iota(wide, 1), mine[0:1], 0.0), axis=1, keepdims=True)
    col_r = jnp.sum(jnp.where(iota(wide, 0) == iota(wide, 1), mine[2:3], 0.0), axis=1, keepdims=True)
    choose[0:HALO, :] = jnp.broadcast_to(col_l, (HALO, CELLS))
    choose[HALO:HALO + BLOCKS, :] = jnp.broadcast_to(column(mine[1:2]), (BLOCKS, CELLS))
    choose[HALO + BLOCKS:, :] = jnp.broadcast_to(col_r, (HALO, CELLS))

    own_obs.wait()
    obs_swap.wait_recv()
    bytes_of(obs_near, obs_send.at[0], obs_recv.at[0]).wait_recv()
    odd = iota((8, CELLS), 0) % 2

    def receivers(cells, base, obs_at):
        block = (cells >> 7) + base - HALF * odd
        lane = jnp.where(cell_of(iota(square, 0)) == (cells & (CELLS - 1)), 1.0, 0.0).astype(bf16)
        values = []
        for p in range(2):
            rows = [obs_at[p, pl.ds(4 * core + s, 1), :] for s in range(4)]
            values.append(jnp.concatenate([rows[r // 2] for r in range(8)], axis=0))
        return block, lane, values

    def scatter(block, lane, values, i):
        at = jnp.tile(block, (8, 1)) == 8 * i + (iota((64, CELLS), 0) >> 3)
        twice = jnp.concatenate([lane, lane], axis=1)
        res = []
        for v in values:
            hi, lo = two(jnp.where(at, jnp.tile(v, (8, 1)), 0.0))
            res.append(dot_t(jnp.concatenate([hi, lo], axis=1), twice))
        return res, dot_t(jnp.where(at, 1.0, 0.0).astype(bf16), lane)

    here = receivers(self_v[2], HALO, obs_own)

    @pl.loop(0, HALF // 8)
    def _(i):
        res, cnt = scatter(*here, i)
        rows = pl.ds(pl.multiple_of(64 * i, 64), 64)
        heard[0, rows, :] = res[0]
        heard[1, rows, :] = res[1]
        count[rows, :] = cnt

    last = HALF // 8 - 1
    for side, base, i in ((0, HALO - BLOCKS, 0), (1, HALO + BLOCKS, last)):
        res, cnt = scatter(*receivers(near[side, 2], base, obs_near.at[side]), i)
        rows = slice(64 * i, 64 * i + 64)
        heard[0, rows, :] += res[0]
        heard[1, rows, :] += res[1]
        count[rows, :] += cnt

    for c in own_src:
        c.wait()
    bytes_of(stage.at[0:4 * BLOCKS, :], ex_send.at[0], ex_recv.at[0]).wait_recv()
    bytes_of(stage.at[0:16 * HALO, :], halo_send.at[0], halo_recv.at[0]).wait_recv()

    even_rows = iota((64, CELLS), 0) % 2 == 0
    keep_l = jnp.where(even_rows & (me == 0), 0.0, 1.0)
    keep_r = jnp.where(jnp.logical_not(even_rows) & (me == nm - 1), 0.0, 1.0)

    def kept(i, x):
        if isinstance(i, int):
            return x * keep_l if i == 0 else x * keep_r if i == last else x
        return x * jnp.where(i == 0, keep_l, jnp.where(i == last, keep_r, 1.0))

    def at64(i, first=0):
        return slice(first + 64 * i, first + 64 * i + 64) if isinstance(i, int) else pl.ds(
            pl.multiple_of(first + 64 * i, 8), 64)

    def put(b, p, i, x):
        b[p, at64(i, 8), :] = x
        hi, lo = two(x)
        lhs_hi[at64(2 * i + p), :] = hi
        lhs_lo[at64(2 * i + p), :] = lo

    def seams(b):
        top = iota((8, CELLS), 0) % 2 == 0
        for p in range(2):
            end = b[p, ROWS:ROWS + 8, :]
            start = b[p, 8:16, :]
            b[p, 0:8, :] = jnp.where(top, 0.0, pltpu.roll(end, 1, axis=0))
            b[p, ROWS + 8:ROWS + 16, :] = jnp.where(top, pltpu.roll(start, 7, axis=0), 0.0)

    @pl.loop(0, HALF // 8)
    def _(i):
        for p in range(2):
            x = jnp.concatenate(
                [stage[pl.ds(p * (4 * STAGE) + 8 * i + j, 8, stride=HALF), :] for j in range(8)], axis=0
            )
            x = kept(i, reorder(x) * dinv)
            q[0, p, at64(i), :] = x
            put(fwd_a, p, i, x)

    seams(fwd_a)

    own_table.wait()
    bytes_of(table.at[0:(nz - 1) * (NX - 1) * half_rows, :], fan_send.at[0], fan_recv.at[1]).wait_recv()
    to_scalars.wait()

    def pick_rows(first, source, lane):
        picked[pl.ds(first, 8), :] = jnp.concatenate(
            [table[pl.ds(index_s[source, lane + j], 1), :] for j in range(8)], axis=0
        )

    def swap_part(k):
        rows = pl.ds(k * (STAGE // 2), STAGE // 2)
        return remote(picked.at[rows, :], theirs.at[rows, :], pick_send.at[0], pick_recv.at[0], c=other)

    for i in range(STAGE // 8):
        source = 0 if i == 0 else 2 if i == STAGE // 8 - 1 else 1
        pick_rows(8 * i, source, (BLOCKS - HALO, 8 * i - HALO, 0)[source])
        if i == STAGE // 16 - 1:
            swap_part(0).start()
    swap_part(1).start()

    for z, x in far:
        m = z_at[z] + x_at[x]
        remote(slots.at[m], slots_in.at[me], sl_send.at[0], sl_recv.at[0], m=m).start()

    swap = bytes_of(picked, pick_send.at[0], pick_recv.at[0])
    swap.wait_recv()
    wsig[...] = OMEGA * jnp.exp(reorder(jnp.where(choose[...] > 0.5, picked[...], theirs[...])))

    for i in range(HALF // 8):
        rows = []
        for j in range(8):
            a = jnp.broadcast_to(wsig[pl.ds(8 * i + j, 1), :], (8, CELLS))
            b = jnp.broadcast_to(wsig[pl.ds(HALF + 8 * i + j, 1), :], (8, CELLS))
            rows.append(jnp.where(odd == 0, a, b))
        cross[at64(i), :] = kept(i, jnp.concatenate(rows, axis=0) * dinv)

    lane_row = iota((1, CELLS), 1)
    ends = jnp.where((lane_row == 0) | (lane_row == CELLS // 2), CHAIN * dinv, 0.0)
    low_lane = iota((64, CELLS), 1) < CELLS // 4

    def sweep(old, new, qk, sign, weights):
        for first, until in GROUPS:
            rows = slice(128 * first, 128 * until)
            prod = dot(jnp.concatenate([lhs_hi[rows, :], lhs_lo[rows, :]], axis=1), weights[...])
            prod = prod[:, 0:CELLS] + prod[:, CELLS:]
            for i in range(first, until):
                turn = cross[at64(i), :]
                near_x = [old[p, 64 * i:64 * i + 80, :] for p in range(2)]
                for p in range(2):
                    k = 2 * (i - first) + p
                    end = jnp.where(low_lane, near_x[p][16:80], near_x[p][0:64])
                    both = turn * near_x[1 - p][8:72]
                    x = q[qk, p, at64(i), :] + ends * pltpu.roll(end, CELLS // 2, axis=1)
                    x = x + both if (sign > 0) == (p == 0) else x - both
                    x = x + prod[64 * k:64 * k + 64, :]
                    put(new, p, i, kept(i, x))
        seams(new)

    def sweeps(a, b, *args):
        sweep(a, b, *args)

        @pl.loop(0, ITERS // 2 - 1)
        def _(k):
            sweep(b, a, *args)
            sweep(a, b, *args)

    sweeps(fwd_a, fwd_b, 0, 1, wf)

    for i in range(HALF // 8):
        for p in range(2):
            x = count[at64(i), :] * fwd_b[p, at64(i, 8), :] - heard[p, at64(i), :]
            x = kept(i, x * dinv)
            q[1, p, at64(i), :] = x
            put(adj_a, p, i, x)

    seams(adj_a)

    sweeps(adj_a, adj_b, 1, -1, wa)

    for i in range(HALF // 8):
        psum_buf[at64(i), :] = (
            adj_b[0, at64(i, 8), :] * fwd_b[1, at64(i, 8), :]
            - adj_b[1, at64(i, 8), :] * fwd_b[0, at64(i, 8), :]
        )

    for i in range(BLOCKS // 16):
        for h in range(2):
            first = 8 * (8 * i + (HALO if h == 0 else 0)) + h
            acc = psum_buf[pl.ds(first, 8, stride=8), :]
            for s in range(1, 4):
                acc = acc + psum_buf[pl.ds(first + 2 * s, 8, stride=8), :]
            at = 8 * i + (HALF - HALO) * h
            part[at:at + 8, :] = acc * wsig[HALO + at:HALO + at + 8, :]

    hi, mid, lo = three(reorder(part[...]))
    sel = qmat[...]
    packed = dot(jnp.concatenate([sel, sel], axis=1), jnp.concatenate([hi, mid], axis=0)) + dot(sel, lo)
    pack[...] = packed.reshape(nm, CAP, CELLS)

    takes = lax.rem(mx + 1, 2) == core
    for z, x in far:
        m = z_at[z] + x_at[x]
        remote(
            pack.at[m], pack_in.at[core * nm + me], gp_send.at[0], gp_recv.at[0], m=m, c=lax.rem(x_at[x] + 1, 2)
        ).start()
    beside_me = remote(pack.at[me], pack_in.at[core * nm + me], gp_send.at[1], gp_recv.at[0], c=other)

    @pl.when(jnp.logical_not(takes))
    def _():
        beside_me.start()

    @pl.when(takes)
    def _():
        pack_in[core * nm + me] = pack[me]

    bytes_of(slots.at[0:nm - 1], sl_send.at[0], sl_recv.at[0]).wait_recv()
    slots_in[me] = slots[me]

    bytes_of(table.at[0:(nz - 1) * half_rows, :], ag_send.at[0], ag_recv.at[0]).wait_send()
    bytes_of(near, small_send.at[0], small_recv.at[0]).wait_send()
    bytes_of(stage.at[0:4 * BLOCKS, :], ex_send.at[0], ex_recv.at[0]).wait_send()
    obs_swap.wait_send()
    bytes_of(stage.at[0:16 * HALO, :], halo_send.at[0], halo_recv.at[0]).wait_send()
    bytes_of(obs_near, obs_send.at[0], obs_recv.at[0]).wait_send()
    bytes_of(table.at[0:nz * (NX - 1) * half_rows, :], fan_send.at[0], fan_recv.at[0]).wait_send()
    swap.wait_send()
    bytes_of(slots.at[0:nm - 1], sl_send.at[0], sl_recv.at[0]).wait_send()

    back = remote(total, total_in, to_send.at[0], to_recv.at[0], c=other)

    @pl.when(takes)
    def _():
        slot_in = slots_in[...].reshape(nm * CAP, CELLS)
        hit = jnp.where(slot_in == (iota((nm * CAP, CELLS), 1) + 1).astype(f32), 1.0, 0.0)
        hits[...] = hit.T.astype(bf16)

        bytes_of(pack_in.at[0:2 * nm - 1], gp_send.at[0], gp_recv.at[0]).wait_recv()
        rows = (pack_in[0:nm] + pack_in[nm:2 * nm]).reshape(nm * CAP, CELLS)
        hi, mid, lo = three(rows)
        sel = hits[0:OWNED, :]
        line[grp] = dot(jnp.concatenate([sel, sel], axis=1), jnp.concatenate([hi, mid], axis=0)) + dot(sel, lo)

        for d in far_g:
            remote(line.at[grp], line.at[grp], ln_send.at[0], ln_recv.at[0], g=g_at[d]).start()
        bytes_of(line.at[0:ng - 1], ln_send.at[0], ln_recv.at[0]).wait_recv()
        summed = line[0]
        for g in range(1, ng):
            summed = summed + line[g]
        total[...] = summed
        back.start()
        out_ref[...] = summed
        bytes_of(line.at[0:ng - 1], ln_send.at[0], ln_recv.at[0]).wait_send()
        back.wait_send()

    @pl.when(jnp.logical_not(takes))
    def _():
        beside_me.wait_send()
        back.wait_recv()
        out_ref[...] = total_in[...]

    bytes_of(pack.at[0:nm - 1], gp_send.at[0], gp_recv.at[0]).wait_send()


def local(log_sigma, block_owner, block_slot, coupling, sources, rcv_cell, observed):
    nm, ng = lax.axis_size("mesh"), lax.axis_size("group")
    vmem, hbm, dma = pltpu.VMEM, pl.BlockSpec(memory_space=pl.ANY), pltpu.SemaphoreType.DMA
    inside = pl.BlockSpec(memory_space=pltpu.VMEM)
    nz = nm // NX
    return pl.pallas_call(
        functools.partial(kernel, ng, nm),
        out_shape=pltpu.VMEM((OWNED, CELLS), f32),
        in_specs=[hbm] * 7,
        out_specs=inside,
        scratch_shapes=[
            vmem((8 * STAGE, CELLS), f32),
            vmem((nm * OWNED // 2, CELLS), f32),
            vmem((2, 3, 1, BLOCKS), i32),
            vmem((3, 1, BLOCKS), i32),
            vmem((CELLS, CELLS), f32),
            vmem((2, S, CELLS), f32),
            vmem((2, 2, S, CELLS), f32),
            vmem((8, BLOCKS), i32),
            pltpu.SMEM((8, BLOCKS), i32),
            vmem((STAGE, CELLS), f32),
            vmem((STAGE, CELLS), f32),
            vmem((STAGE, CELLS), f32),
            vmem((2, ROWS + 16, CELLS), f32),
            vmem((2, ROWS + 16, CELLS), f32),
            vmem((2, ROWS + 16, CELLS), f32),
            vmem((2, ROWS + 16, CELLS), f32),
            vmem((2 * ROWS, CELLS), bf16),
            vmem((2 * ROWS, CELLS), bf16),
            vmem((2, 2, ROWS, CELLS), f32),
            vmem((ROWS, CELLS), f32),
            vmem((STAGE, CELLS), f32),
            vmem((CELLS, nm * CAP), bf16),
            vmem((2, ROWS, CELLS), f32),
            vmem((ROWS, CELLS), f32),
            vmem((2 * CELLS, 2 * CELLS), bf16),
            vmem((2 * CELLS, 2 * CELLS), bf16),
            vmem((nm * CAP, BLOCKS), bf16),
            vmem((ROWS, CELLS), f32),
            vmem((BLOCKS, CELLS), f32),
            vmem((nm, CAP, CELLS), f32),
            vmem((nm, CAP, CELLS), f32),
            vmem((nm, CAP, CELLS), f32),
            vmem((2 * nm, CAP, CELLS), f32),
            vmem((ng, OWNED, CELLS), f32),
            vmem((OWNED, CELLS), f32),
            vmem((OWNED, CELLS), f32),
            dma((10,)),
            dma((2,)), dma((2,)),
            dma((1,)), dma((1,)),
            dma((1,)), dma((1,)),
            dma((1,)), dma((1,)),
            dma((1,)), dma((nz,)),
            dma((1,)), dma((2,)),
            dma((1,)), dma((1,)),
            dma((1,)), dma((1,)),
            dma((2,)), dma((1,)),
            dma((1,)), dma((1,)),
            dma((1,)), dma((1,)),
            dma(()),
        ],
        compiler_params=pltpu.CompilerParams(collective_id=0, has_side_effects=True),
    )(
        block_owner.reshape(1, BLOCKS), block_slot, rcv_cell, observed.reshape(S, CELLS), coupling, log_sigma, sources.reshape(S, BLOCKS, CELLS)
    )


def solution(mesh):
    in_specs = (
        P("mesh", None),
        P("group", "mesh", None),
        P("group", "mesh"),
        P(),
        P("group", "comp", None, "mesh", None),
        P("group", "mesh"),
        P("group", "comp", None, "mesh"),
    )
    return jax.shard_map(local, mesh=mesh, in_specs=in_specs, out_specs=P("mesh", None), check_vma=False)
```
